32 devices in a mesh: groups: 2 (over y), wide: 4 (over z), planes: 2 (over x), rep: 2 (over core).
Axes of the slice: x: 2, y: 2, z: 4, core: 2. Of those that a mesh axis runs over, the one named last changes fastest.
Arguments:
- movie_frames: bfloat16 [4, 128, 256, 128], P('planes', ('groups', 'wide'), 'rep'), parts along dimension 1, may hold values from -6 to 6
- pixel_mask: int32 [256, 128], P('rep'), may hold values 0 or 1
- tile_owner: int32 [256, 1], P('rep'), may hold values from 0 to 3; in each aligned block of 128 rows (0 to 127, 128 to 255, ...) at most 48 rows name the same one
- support: int32 [256, 128], P('rep'), may hold values from 0 to 511
- templates: bfloat16 [512, 4, 128], P(None, 'planes'), may hold values from -0.25 to 0.25
- row_taps: float32 [25], replicated, may hold values from -1.25 to 1.25
- col_taps: float32 [25], replicated, may hold values from -1.25 to 1.25
- lag_gains: float32 [4, 3, 65], P('wide'), may hold values from -0.4375 to 0.4375
- dilations: int32 [4, 3], P('wide'), may hold values from 1 to 8
Outputs:
- traces: bfloat16 [128, 128, 256], P('planes', ('groups', 'wide'), 'rep'), parts along dimension 1
- back_projected: bfloat16 [4, 128, 256, 128], P('planes', ('groups', 'wide'), 'rep'), parts along dimension 1
The draws below stay inside these ranges and needn't reach their ends.
There are 2 independent parts, one for each index of `groups`. The reference program is written for one: setup_inputs(seed, part) draws one part's arguments, and reference() takes and returns one part's arrays. A program takes and returns all parts, laid end to end along the dimension named above; an argument that names none is the same for every part. Nothing has to cross between parts.
Inputs may be any that keep to these rules, and one draw needn't show every extreme that they name: Strip h belongs to region class tile_owner[h,0]; the 128 rows of one device name each class at most 48 times.
All inputs are finite; a program needn't handle non-finite values. No bound on the sum of `pixel_mask` on one device may be relied on, other than what follows from the above.
Results may differ from the reference program's by a relative error of at most 0.015.
Values may be sent and summed in bfloat16 or wider, within the bound.
A program may use at most 64 MiB of HBM per device.

```python
import math
import jax
import jax.numpy as jnp
import numpy as np
from jax import lax

H = 256
W = 128
FP = 128
NCOMP = 512
TAPS_S = 25
TAPS_T = 65
BANDS = 3
DMAX = 8
PLANES = 4
FRAMES = 64
HH = 128
CLUSTERS = 4
CAP = 48
N_REP = 2


def place_ends(entries, stream_key, least, high):
    longest = entries.shape.index(max(entries.shape))
    spots = []
    for shift in (0, 1):
        where = [jax.random.randint(jax.random.fold_in(stream_key, axis), (), 0, length) for axis, length in enumerate(entries.shape)]
        where[longest] = (where[longest] + shift) % entries.shape[longest]
        spots.append(tuple(where))
    return entries.at[spots[0]].set(least).at[spots[1]].set(high)


def level_of(key, shape, shards, smallest, top_value):
    def one(position, shards_of):
        draws = jax.random.uniform(jax.random.fold_in(jax.random.fold_in(key, 6), position), (shards_of,), jnp.float32, smallest / len(shards), top_value / len(shards))
        return jnp.repeat(jnp.exp(draws), shape[position] // shards_of).reshape((-1,) + (1,) * (len(shape) - position - 1))

    factor_of = one(*shards[0])
    for cut in shards[1:]:
        factor_of = factor_of * one(*cut)
    return factor_of


def deal_out(stream_key, own, number, rows, count, top, most, slope):
    sequence = jax.random.permutation(stream_key, count)
    packed, ordinary = load_shares(count, rows * top, most, slope, True), load_shares(count, rows * top, most, slope, False)
    places = jnp.arange(count)

    def named(tallies, offset_by):
        used = int((tallies > 0).sum())
        fixed = max(1, used // 4)
        passed = fixed + (places - fixed + offset_by * (used - fixed)) % max(1, count - fixed)
        return jnp.zeros((count,), jnp.int32).at[sequence[jnp.where(places < fixed, places, passed)]].set(jnp.asarray(tallies, jnp.int32))

    tallies = jnp.where(number % 4 == 0, named(packed, number // 4), named(ordinary, number - number // 4 - 1))
    mixed = jax.random.permutation(jax.random.fold_in(own, 3), count)
    donor, taker = mixed[0:count // 2 * 2:2], mixed[1:count // 2 * 2:2]
    room = jnp.minimum(tallies[donor] - 1, most - tallies[taker]) // 2
    room = jnp.where((donor == sequence[0]) | (taker == sequence[0]) | (tallies[taker] == 0), 0, jnp.maximum(room, 0))
    passed = jax.random.randint(jax.random.fold_in(own, 4), (count // 2,), 0, 1 << 20) % (room + 1)
    tallies = tallies.at[donor].add(-passed).at[taker].add(passed)
    items = jnp.searchsorted(jnp.cumsum(tallies), jnp.arange(rows * top), side="right").astype(jnp.int32)
    grid = items.reshape(top, rows).T
    grid = grid[jax.random.permutation(jax.random.fold_in(own, 1), rows)]
    offset_by = jax.random.randint(jax.random.fold_in(own, 2), (rows, 1), 0, top)
    return jnp.take_along_axis(grid, (jnp.arange(top)[None, :] + offset_by) % top, axis=1)


def load_shares(number_of, total, most, lean, full):
    weights = [(1 << 20) // math.isqrt(grade ** lean) + 1 for grade in range(1, number_of + 1)]
    largest = most if full else min(most, max(-(-total // number_of), total * weights[0] // sum(weights)))
    least = 1 if total - largest >= number_of - 1 else 0
    holding, spare = [largest] + [least] * (number_of - 1), total - largest - least * (number_of - 1)
    while spare > 0:
        free = [i for i in range(1, number_of) if holding[i] < largest] or [i for i in range(1, number_of) if holding[i] < most]
        pool, remaining = sum([weights[i] for i in free]), spare
        for i in free:
            addition = min(most - holding[i], max(1, remaining * weights[i] // pool), spare)
            holding[i] = holding[i] + addition
            spare = spare - addition
    return np.array(holding)


def normal_values(rng, extent, scale, reach, shards=(), held_as=jnp.bfloat16):
    values = scale * jax.random.normal(rng, extent, jnp.float32)
    if shards:
        values = values * level_of(rng, extent, shards, -0.22, 0.18)
    return jnp.clip(values, -reach, reach).astype(held_as)


def setup_inputs(seed: int = 0, part: int = 0) -> dict:
    key_list = jax.random.split(jax.random.key(seed), 10)
    own_keys = jax.random.split(jax.random.fold_in(key_list[9], part), 10)
    movie_frames = normal_values(own_keys[0], (PLANES, FRAMES, H, W), 1.0, 6.0, ((0, 2), (1, 4), (2, 2)))
    pixel_mask = place_ends((jax.random.randint(key_list[1], (H, W), 0, 4) < 3).astype(jnp.int32), jax.random.fold_in(key_list[1], 1), 0, 1)
    tile_owner_keys = jax.random.split(jax.random.fold_in(key_list[2], 1), H // HH)
    tile_owner_turns = jax.random.permutation(jax.random.fold_in(key_list[2], 3), H // HH)
    tile_owner = jax.vmap(lambda own, number: deal_out(jax.random.fold_in(key_list[2], 2), own, number, HH, CLUSTERS, 1, CAP, 2))(tile_owner_keys, tile_owner_turns).reshape((H, 1))
    support = place_ends(jax.random.randint(key_list[3], (H, FP), 0, NCOMP), jax.random.fold_in(key_list[3], 1), 0, NCOMP - 1).astype(jnp.int32)
    templates = normal_values(key_list[4], (NCOMP, PLANES, W), (PLANES * W) ** -0.5, 0.25, ((1, 2),))
    row_taps = normal_values(key_list[5], (TAPS_S,), TAPS_S ** -0.5, 1.25, (), jnp.float32)
    col_taps = normal_values(key_list[6], (TAPS_S,), TAPS_S ** -0.5, 1.25, (), jnp.float32)
    lag_gains = normal_values(key_list[7], (CLUSTERS, BANDS, TAPS_T), (BANDS * TAPS_T) ** -0.5, 0.4375, ((0, 4),), jnp.float32)
    dilations = place_ends(jax.random.randint(key_list[8], (CLUSTERS, BANDS), 1, DMAX + 1), jax.random.fold_in(key_list[8], 1), 1, DMAX).astype(jnp.int32)
    return {"movie_frames": movie_frames, "pixel_mask": pixel_mask, "tile_owner": tile_owner, "support": support, "templates": templates, "row_taps": row_taps, "col_taps": col_taps, "lag_gains": lag_gains, "dilations": dilations}


def band_matrix(tap_values, rows_in, rows_out, sign, offset):
    inner_idx = jnp.arange(rows_in, dtype=jnp.int32)[:, None]
    outer_idx = jnp.arange(rows_out, dtype=jnp.int32)[None, :]
    where_tap = sign * (inner_idx - outer_idx) + offset
    tap_index = jnp.arange(tap_values.shape[0], dtype=jnp.int32)
    picked_taps = where_tap[:, :, None] == tap_index[None, None, :]
    weights = jnp.where(picked_taps, tap_values[None, None, :], jnp.zeros((), tap_values.dtype))
    return jnp.sum(weights, axis=2).astype(jnp.bfloat16)


def lag_matrix(cluster_gains, cluster_lags, frame_count):
    tap_count = cluster_gains.shape[1]
    half_taps = (tap_count - 1) // 2
    lag_values = jnp.arange(2 * frame_count - 1, dtype=jnp.int32) - (frame_count - 1)
    tap_offsets = jnp.arange(tap_count, dtype=jnp.int32) - half_taps
    lag_hits = lag_values[None, :, None] == cluster_lags[:, None, None] * tap_offsets[None, None, :]
    spread = jnp.where(lag_hits, cluster_gains[:, None, :], jnp.zeros((), cluster_gains.dtype))
    kernel = jnp.sum(spread, axis=(0, 2))
    flipped = jnp.concatenate([kernel[::-1], jnp.zeros((1,), kernel.dtype)])
    tiled = jnp.broadcast_to(flipped, (frame_count, 2 * frame_count)).reshape(-1)
    tiled = tiled[: frame_count * (2 * frame_count - 1)].reshape(frame_count, 2 * frame_count - 1)
    return tiled[:, frame_count - 1:].astype(jnp.bfloat16)


def slot_table(owners, cluster_count, capacity):
    row_count = owners.shape[0]
    owner_marks = (owners[:, None] == jnp.arange(cluster_count, dtype=jnp.int32)[None, :]).astype(jnp.int32)
    before = jnp.cumsum(owner_marks, axis=0) - owner_marks
    slot_ranks = jnp.sum(before * owner_marks, axis=1)
    slot_of = owners * capacity + slot_ranks
    places = jnp.arange(cluster_count * capacity, dtype=jnp.int32)
    chosen = (slot_of[None, :] == places[:, None]).astype(jnp.int32)
    sources = jnp.sum(chosen * jnp.arange(row_count, dtype=jnp.int32)[None, :], axis=1)
    return slot_of, sources


def reference(movie_frames, pixel_mask, tile_owner, support, templates, row_taps, col_taps, lag_gains, dilations):
    plane_count, frame_count, row_count, col_count = movie_frames.shape
    half_rows = row_count // N_REP
    rim_width = (row_taps.shape[0] - 1) // 2
    col_fwd = band_matrix(col_taps, col_count, col_count, 1, rim_width)
    row_fwd = band_matrix(row_taps, row_count, row_count, 1, rim_width)
    col_adj = band_matrix(col_taps, col_count, col_count, -1, rim_width)
    row_adj = band_matrix(row_taps, row_count, row_count, -1, rim_width)
    mask_value = pixel_mask.astype(jnp.float32)

    def forward_plane(plane_frames):
        smooth = jnp.dot(plane_frames, col_fwd, preferred_element_type=jnp.float32).astype(jnp.bfloat16)
        along = jnp.einsum('thw,hg->tgw', smooth.astype(jnp.float32), row_fwd.astype(jnp.float32), precision=lax.Precision.HIGHEST)
        return (along * mask_value[None]).astype(jnp.bfloat16)

    filtered = lax.map(forward_plane, movie_frames)

    owner_halves = tile_owner[:, 0].reshape(N_REP, half_rows)
    slot_parts = []
    source_parts = []
    for half_index in range(N_REP):
        slot_of, sources = slot_table(owner_halves[half_index], CLUSTERS, CAP)
        slot_parts.append(slot_of)
        source_parts.append(sources + half_index * half_rows)
    picked_all = jnp.stack(source_parts).reshape(N_REP, CLUSTERS, CAP)
    picked_all = jnp.transpose(picked_all, (1, 0, 2)).reshape(CLUSTERS, N_REP * CAP).astype(jnp.int32)

    def per_cluster(inputs):
        cluster_gains, cluster_lags, picked = inputs
        lag_table = lag_matrix(cluster_gains, cluster_lags, frame_count)
        columns = jnp.take(filtered, picked, axis=2)
        mixed_cols = jnp.einsum('pscw,st->ptcw', columns.astype(jnp.float32), lag_table.astype(jnp.float32), precision=lax.Precision.HIGHEST).astype(jnp.bfloat16)
        shapes = jnp.take(templates, jnp.take(support, picked, axis=0), axis=0)
        scores = jnp.einsum('cjpw,ptcw->cjt', shapes.astype(jnp.float32), mixed_cols.astype(jnp.float32), precision=lax.Precision.HIGHEST)
        return jnp.maximum(scores, 0.0).astype(jnp.bfloat16)

    cluster_traces = lax.map(per_cluster, (lag_gains, dilations, picked_all))
    foot_count = cluster_traces.shape[2]
    flat_parts = []
    for half_index in range(N_REP):
        owners_here = owner_halves[half_index]
        slot_ranks = slot_parts[half_index] - owners_here * CAP
        flat_parts.append(owners_here * (N_REP * CAP) + half_index * CAP + slot_ranks)
    flat_index = jnp.concatenate(flat_parts).astype(jnp.int32)
    flat_traces = cluster_traces.reshape(CLUSTERS * N_REP * CAP, foot_count, frame_count)
    tile_traces = jnp.take(flat_traces, flat_index, axis=0)

    tile_shapes = jnp.take(templates, support, axis=0)
    plane_shapes = jnp.transpose(tile_shapes, (2, 0, 1, 3))
    trace_value = tile_traces.astype(jnp.float32)

    def backward_plane(inputs):
        plane_filtered, shape_plane = inputs
        model_part = jnp.einsum('hjw,hjt->thw', shape_plane.astype(jnp.float32), trace_value, precision=lax.Precision.HIGHEST)
        residual = (plane_filtered.astype(jnp.float32) - mask_value[None] * model_part).astype(jnp.bfloat16)
        back_rows = jnp.einsum('thw,hg->tgw', residual.astype(jnp.float32), row_adj.astype(jnp.float32), precision=lax.Precision.HIGHEST).astype(jnp.bfloat16)
        return jnp.dot(back_rows, col_adj, preferred_element_type=jnp.float32).astype(jnp.bfloat16)

    back_projected = lax.map(backward_plane, (filtered, plane_shapes))
    traces = jnp.transpose(tile_traces, (1, 2, 0))
    return traces, back_projected
```

```python
import jax
import jax.numpy as jnp
from jax import lax
from jax.experimental import pallas as pl
from jax.experimental.pallas import tpu as pltpu
from jax.sharding import PartitionSpec as P

MESH = pl.DeviceIdType.MESH
BF = jnp.bfloat16
F32 = jnp.float32
I32 = jnp.int32
LANES = 128
TILE = 16


def iota(shape, dim):
    return lax.broadcasted_iota(I32, shape, dim)


def from_taps(tap_ref, where_tap):
    weights = jnp.zeros(where_tap.shape, F32)
    for k in range(tap_ref.shape[0]):
        weights = jnp.where(where_tap == k, tap_ref[k], weights)
    return weights.astype(BF)


def whole_kernel(
    movie_hbm, temp_hbm, sup_ref, mask_ref, own_ref, row_ref, col_ref, gain_ref, dil_ref,
    tr_hbm, back_hbm,
    movie, temp_raw, temp32, temp, temp_t, col_fwd, col_adj, row_fwd, row_adj, lag_own,
    smooth, resid, fbuf, pall, part, xrecv, zsend, gath, lag_all, tbuf, tr_all, tr32, tt32, fold,
    tr_out, back_out,
    in_s, out_s, h1_s, h1_r, h2_s, h2_r,
    lag_s, lag_r, x1_s, x1_r, z1_s, z1_r, z2_s, z2_r, x2_s, x2_r,
):
    np_ = lax.axis_size("planes")
    nw = lax.axis_size("wide")
    nr = lax.axis_size("rep")
    p = lax.axis_index("planes")
    z = lax.axis_index("wide")
    r = lax.axis_index("rep")
    planes, frames, rows, cols = movie.shape
    pixels = planes * cols
    blocks, hb, _, comps = part.shape
    shapes = temp.shape[0]
    total = nw * frames
    pad = (smooth.shape[1] - rows) // 2
    rim = (row_ref.shape[0] - 1) // 2
    col_rim = (col_ref.shape[0] - 1) // 2

    barrier = pltpu.get_barrier_semaphore()
    for k in range(1, nw):
        pl.semaphore_signal(barrier, inc=1, device_id={"wide": lax.rem(z + k, nw)}, device_id_type=MESH)
    for k in range(1, np_):
        pl.semaphore_signal(barrier, inc=1, device_id={"planes": lax.rem(p + k, np_)}, device_id_type=MESH)

    @pl.when(r > 0)
    def _():
        pl.semaphore_signal(barrier, inc=1, device_id={"rep": r - 1}, device_id_type=MESH)

    @pl.when(r < nr - 1)
    def _():
        pl.semaphore_signal(barrier, inc=1, device_id={"rep": r + 1}, device_id_type=MESH)

    movie_in = pltpu.make_async_copy(movie_hbm, movie, in_s.at[0])
    temp_in = pltpu.make_async_copy(temp_hbm, temp_raw, in_s.at[1])
    movie_in.start()
    temp_in.start()

    col_fwd[...] = jnp.zeros(col_fwd.shape, BF)
    col_adj[...] = jnp.zeros(col_adj.shape, BF)
    gap = iota((cols, cols), 0) - iota((cols, cols), 1)
    fwd_block = from_taps(col_ref, gap + col_rim)
    for q in range(planes):
        side = slice(q * cols, (q + 1) * cols)
        col_fwd[side, side] = fwd_block

    zeros = jnp.zeros((frames, pad, pixels), BF)

    @pl.when(r == 0)
    def _():
        smooth[:, :pad, :] = zeros
        resid[:, :pad, :] = zeros

    @pl.when(r == nr - 1)
    def _():
        smooth[:, pad + rows :, :] = zeros
        resid[:, pad + rows :, :] = zeros

    movie_in.wait()
    step = max(1, min(frames, 512 // rows))
    for f in range(0, frames, step):
        x = jnp.concatenate([movie[q, f : f + step].reshape(step * rows, cols) for q in range(planes)], axis=1)
        y = jnp.dot(x, col_fwd[...], preferred_element_type=F32).astype(BF)
        smooth[f : f + step, pad : pad + rows, :] = y.reshape(step, rows, pixels)

    edge = iota((rows, rows + 2 * pad), 1) - iota((rows, rows + 2 * pad), 0) - pad
    row_fwd[...] = from_taps(row_ref, edge + rim)

    taps_t = gain_ref.shape[1]
    wide_lags = 2 * total
    lag = iota((taps_t, wide_lags), 1) - (total - 1)
    offset = iota((taps_t, wide_lags), 0) - (taps_t - 1) // 2
    kern = jnp.zeros((1, wide_lags), F32)
    for b in range(gain_ref.shape[0]):
        hits = jnp.where(lag == dil_ref[b] * offset, 1.0, 0.0)
        kern = kern + jnp.dot(
            gain_ref[b : b + 1, :], hits, precision=lax.Precision.HIGHEST, preferred_element_type=F32)
    kern = jnp.broadcast_to(kern, (TILE, wide_lags))
    for t in range(0, total, TILE):
        turned = pltpu.roll(kern, (total + 1 + t) % wide_lags, 1, stride=1, stride_axis=0)
        lag_own[t : t + TILE, :] = turned[:, :total].astype(BF)

    pl.semaphore_wait(
        barrier, nw - 1 + np_ - 1 + (r > 0).astype(I32) + (r < nr - 1).astype(I32))

    def halo_down(ext, send, recv):
        return pltpu.make_async_remote_copy(
            src_ref=ext.at[:, pl.ds(rows, pad), :], dst_ref=ext.at[:, pl.ds(0, pad), :],
            send_sem=send.at[0], recv_sem=recv.at[0],
            device_id={"rep": lax.rem(r + 1, nr)}, device_id_type=MESH)

    def halo_up(ext, send, recv):
        return pltpu.make_async_remote_copy(
            src_ref=ext.at[:, pl.ds(pad, pad), :], dst_ref=ext.at[:, pl.ds(rows + pad, pad), :],
            send_sem=send.at[1], recv_sem=recv.at[1],
            device_id={"rep": lax.rem(r + nr - 1, nr)}, device_id_type=MESH)

    def halo_start(ext, send, recv):
        @pl.when(r < nr - 1)
        def _():
            halo_down(ext, send, recv).start()

        @pl.when(r > 0)
        def _():
            halo_up(ext, send, recv).start()

    def halo_wait(ext, send, recv):
        @pl.when(r < nr - 1)
        def _():
            halo_down(ext, send, recv).wait_send()
            halo_up(ext, send, recv).wait_recv()

        @pl.when(r > 0)
        def _():
            halo_up(ext, send, recv).wait_send()
            halo_down(ext, send, recv).wait_recv()

    halo_start(smooth, h1_s, h1_r)

    def to_wide(src, dst, send, recv, k):
        return pltpu.make_async_remote_copy(
            src_ref=src, dst_ref=dst, send_sem=send.at[k - 1], recv_sem=recv.at[k - 1],
            device_id={"wide": lax.rem(z + k, nw)}, device_id_type=MESH)

    def to_plane(src, dst, send, recv, dp, zi):
        slot = (dp - 1) * nw + zi
        return pltpu.make_async_remote_copy(
            src_ref=src, dst_ref=dst, send_sem=send.at[slot], recv_sem=recv.at[slot],
            device_id={"planes": lax.rem(p + dp, np_)}, device_id_type=MESH)

    def lag_copy(k):
        return to_wide(lag_own, lag_all.at[z], lag_s, lag_r, k)

    def x1_copy(dp, zi):
        return to_plane(part.at[lax.rem(p + dp, np_) * nw + zi], xrecv.at[(dp - 1) * nw + zi], x1_s, x1_r, dp, zi)

    def z1_copy(k):
        return to_wide(zsend.at[lax.rem(z + k, nw)], gath.at[z], z1_s, z1_r, k)

    def z2_copy(k):
        return to_wide(tbuf.at[lax.rem(z + k, nw)], tr_all.at[p * nw + z], z2_s, z2_r, k)

    def x2_copy(dp, zi):
        return to_plane(tr_all.at[p * nw + zi], tr_all.at[p * nw + zi], x2_s, x2_r, dp, zi)

    for k in range(1, nw):
        lag_copy(k).start()
    lag_all[z] = lag_own[...]

    temp_in.wait()
    temp32[...] = temp_raw[...].astype(F32)
    for q in range(planes):
        side = slice(q * cols, (q + 1) * cols)
        one = temp32[pl.ds(q, shapes, stride=planes), :]
        temp[:, side] = one.astype(BF)
        temp_t[side, :] = jnp.transpose(one).astype(BF)

    mask = mask_ref[...].astype(F32)
    halo_wait(smooth, h1_s, h1_r)
    for f in range(frames):
        along = jnp.dot(row_fwd[...], smooth[f], preferred_element_type=F32)
        for q in range(planes):
            one = along[:, q * cols : (q + 1) * cols] * mask
            fbuf[q, pl.ds(f, rows, stride=frames), :] = one.astype(BF).astype(F32)

    def project(b):
        base = pl.multiple_of(b * hb, hb)
        lines = pl.ds(pl.multiple_of(b * hb * frames, hb * frames), hb * frames)
        x = jnp.concatenate([fbuf[q, lines, :].astype(BF) for q in range(planes)], axis=1)
        pall[...] = jnp.dot(x, temp_t[...], preferred_element_type=F32)
        sup = sup_ref[pl.ds(base, hb), :]
        low = lax.rem(sup, LANES)
        high = lax.div(sup, LANES)
        for i in range(hb):
            lo = jnp.broadcast_to(low[i : i + 1, :], (frames, comps))
            hi = jnp.broadcast_to(high[i : i + 1, :], (frames, comps))
            got = jnp.zeros((frames, comps), F32)
            for q in range(shapes // LANES):
                piece = pall[i * frames : (i + 1) * frames, q * LANES : (q + 1) * LANES]
                picked = jnp.take_along_axis(piece, lo, axis=1, mode="promise_in_bounds")
                got = jnp.where(hi == q, picked, got)
            part[b, i] = got.astype(BF)

    def others(n, carry):
        dp = n // nw + 1
        zi = lax.rem(z + 1 + lax.rem(n, nw), nw)
        project(lax.rem(p + dp, np_) * nw + zi)
        x1_copy(dp, zi).start()
        return carry

    lax.fori_loop(0, (np_ - 1) * nw, others, 0)

    def mine(n, carry):
        zi = lax.rem(z + 1 + n, nw)
        b = p * nw + zi
        project(b)
        acc = part[b].astype(F32)
        for dp in range(1, np_):
            x1_copy(dp, zi).wait_recv()
            acc = acc + xrecv[(dp - 1) * nw + zi].astype(F32)
        zsend[zi] = acc.astype(BF)

        @pl.when(n < nw - 1)
        def _():
            z1_copy(n + 1).start()

        return carry

    lax.fori_loop(0, nw, mine, 0)
    gath[z] = zsend[z]

    row_adj[...] = from_taps(row_ref, rim - edge)
    adj_block = from_taps(col_ref, col_rim - gap)
    for q in range(planes):
        side = slice(q * cols, (q + 1) * cols)
        col_adj[side, side] = adj_block

    def arrived(k, carry):
        lag_copy(k).wait()
        z1_copy(k).wait()
        return carry

    lax.fori_loop(1, nw, arrived, 0)

    me = p * nw + z
    for i in range(hb):
        table = lag_all[own_ref[me * hb + i]]
        columns = gath[:, i].reshape(total, comps)
        scores = jnp.dot(table, columns, preferred_element_type=F32)
        tbuf[:, i] = jnp.maximum(scores, 0.0).astype(BF).reshape(nw, frames, comps)

    def give(k, carry):
        z2_copy(k).start()
        return carry

    lax.fori_loop(1, nw, give, 0)
    tr_all[me] = tbuf[z]

    tile = min(256, shapes)
    groups = tile // TILE
    ids = (iota((groups, TILE, comps), 0) * TILE + iota((groups, TILE, comps), 1)).astype(F32).astype(BF)

    def model(b):
        base = pl.multiple_of(b * hb, hb)
        first = pl.multiple_of(b * hb * frames, hb * frames)
        sup = sup_ref[pl.ds(base, hb), :]
        for i in range(hb):
            now = tr_all[b, i]
            tr32[pl.ds(first + i * frames, frames), :] = now.astype(F32)
            for q in range(0, shapes, tile):
                row = (sup[i : i + 1, :] - q).astype(F32)
                row = jnp.broadcast_to(row, (TILE, comps)).astype(BF)
                hot = jnp.where(ids == row[None], jnp.ones((), BF), jnp.zeros((), BF)).reshape(tile, comps)
                fold[i * frames : (i + 1) * frames, q : q + tile] = lax.dot_general(
                    now, hot, (((1,), (1,)), ((), ())), preferred_element_type=F32).astype(BF)
        out = jnp.dot(fold[...], temp[...], preferred_element_type=F32)
        lines = pl.ds(first, hb * frames)
        for q in range(planes):
            fbuf[q, lines, :] = fbuf[q, lines, :] - out[:, q * cols : (q + 1) * cols]

    def same_plane(k, carry):
        zi = lax.rem(z + nw - k, nw)

        @pl.when(k > 0)
        def _():
            z2_copy(lax.max(k, 1)).wait_recv()

        for dp in range(1, np_):
            x2_copy(dp, zi).start()
        model(p * nw + zi)
        return carry

    lax.fori_loop(0, nw, same_plane, 0)

    def other_planes(n, carry):
        dp = n // nw + 1
        zi = lax.rem(z + nw - lax.rem(n, nw), nw)
        x2_copy(dp, zi).wait_recv()
        model(lax.rem(p + np_ - dp, np_) * nw + zi)
        return carry

    lax.fori_loop(0, (np_ - 1) * nw, other_planes, 0)

    for f in range(frames):
        for q in range(planes):
            one = fbuf[q, pl.ds(f, rows, stride=frames), :] * mask
            resid[f, pad : pad + rows, q * cols : (q + 1) * cols] = one.astype(BF)
    halo_start(resid, h2_s, h2_r)

    share = tr_out.shape[0]
    chosen = iota((share, comps), 1) == iota((share, comps), 0) + p * share
    chosen = jnp.where(chosen, 1.0, 0.0).astype(BF)
    for f in range(frames):
        one = tr32[pl.ds(f, rows, stride=frames), :].astype(BF)
        tt32[pl.ds(f, share, stride=frames), :] = lax.dot_general(
            chosen, one, (((1,), (1,)), ((), ())), preferred_element_type=F32)
    tr_out[...] = tt32[...].astype(BF).reshape(share, frames, rows)
    tr_copy = pltpu.make_async_copy(tr_out, tr_hbm, out_s.at[0])
    tr_copy.start()

    halo_wait(resid, h2_s, h2_r)
    step = max(1, frames // 4)
    copies = []
    for f0 in range(0, frames, step):
        for f in range(f0, f0 + step):
            y = jnp.dot(row_adj[...], resid[f], preferred_element_type=F32).astype(BF)
            y = jnp.dot(y, col_adj[...], preferred_element_type=F32).astype(BF)
            for q in range(planes):
                back_out[q, f] = y[:, q * cols : (q + 1) * cols]
        copy = pltpu.make_async_copy(
            back_out.at[:, pl.ds(f0, step)], back_hbm.at[:, pl.ds(f0, step)], out_s.at[1 + f0 // step])
        copy.start()
        copies.append(copy)

    def drained_planes(n, carry):
        x1_copy(n // nw + 1, lax.rem(n, nw)).wait_send()
        x2_copy(n // nw + 1, lax.rem(n, nw)).wait_send()
        return carry

    lax.fori_loop(0, (np_ - 1) * nw, drained_planes, 0)

    def drained_wide(k, carry):
        z2_copy(k).wait_send()
        return carry

    lax.fori_loop(1, nw, drained_wide, 0)
    tr_copy.wait()
    for copy in copies:
        copy.wait()


def on_device(
    movie_frames, pixel_mask, tile_owner, support, templates, row_taps, col_taps, lag_gains, dilations
):
    planes, frames, rows, cols = movie_frames.shape
    np_ = lax.axis_size("planes")
    nw = lax.axis_size("wide")
    blocks = np_ * nw
    hb = rows // blocks
    comps = support.shape[1]
    shapes = templates.shape[0]
    total = nw * frames
    pixels = planes * cols
    rim = (row_taps.shape[0] - 1) // 2
    pad = -(-rim // TILE) * TILE
    share = comps // np_
    piece = (hb, frames, comps)
    hbm = pl.BlockSpec(memory_space=pl.ANY)
    vm = pl.BlockSpec(memory_space=pltpu.VMEM)
    sm = pl.BlockSpec(memory_space=pltpu.SMEM)
    dma = pltpu.SemaphoreType.DMA
    traces, back = pl.pallas_call(
        whole_kernel,
        out_shape=(
            jax.ShapeDtypeStruct((share, frames, rows), BF),
            jax.ShapeDtypeStruct(movie_frames.shape, BF),
        ),
        in_specs=[hbm, hbm, vm, vm, sm, sm, sm, vm, sm],
        out_specs=(hbm, hbm),
        scratch_shapes=[
            pltpu.VMEM(movie_frames.shape, BF),
            pltpu.VMEM((shapes * planes, cols), BF),
            pltpu.VMEM((shapes * planes, cols), F32),
            pltpu.VMEM((shapes, pixels), BF),
            pltpu.VMEM((pixels, shapes), BF),
            pltpu.VMEM((pixels, pixels), BF),
            pltpu.VMEM((pixels, pixels), BF),
            pltpu.VMEM((rows, rows + 2 * pad), BF),
            pltpu.VMEM((rows, rows + 2 * pad), BF),
            pltpu.VMEM((total, total), BF),
            pltpu.VMEM((frames, rows + 2 * pad, pixels), BF),
            pltpu.VMEM((frames, rows + 2 * pad, pixels), BF),
            pltpu.VMEM((planes, rows * frames, cols), F32),
            pltpu.VMEM((hb * frames, shapes), F32),
            pltpu.VMEM((blocks,) + piece, BF),
            pltpu.VMEM(((np_ - 1) * nw,) + piece, BF),
            pltpu.VMEM((nw,) + piece, BF),
            pltpu.VMEM((nw,) + piece, BF),
            pltpu.VMEM((nw, total, total), BF),
            pltpu.VMEM((nw,) + piece, BF),
            pltpu.VMEM((blocks,) + piece, BF),
            pltpu.VMEM((rows * frames, comps), F32),
            pltpu.VMEM((share * frames, rows), F32),
            pltpu.VMEM((hb * frames, shapes), BF),
            pltpu.VMEM((share, frames, rows), BF),
            pltpu.VMEM(movie_frames.shape, BF),
            dma((2,)), dma((5,)), dma((2,)), dma((2,)), dma((2,)), dma((2,)),
            dma((nw - 1,)), dma((nw - 1,)),
            dma(((np_ - 1) * nw,)), dma(((np_ - 1) * nw,)),
            dma((nw - 1,)), dma((nw - 1,)),
            dma((nw - 1,)), dma((nw - 1,)),
            dma(((np_ - 1) * nw,)), dma(((np_ - 1) * nw,)),
        ],
        compiler_params=pltpu.CompilerParams(
            collective_id=0, has_side_effects=True, vmem_limit_bytes=60 * 1024 * 1024
        ),
    )(
        movie_frames, templates.reshape(shapes * planes, cols), support, pixel_mask, tile_owner[:, 0],
        row_taps, col_taps, lag_gains[0], dilations[0],
    )
    return traces, back


def solution(mesh):
    return jax.shard_map(
        on_device,
        mesh=mesh,
        in_specs=(
            P("planes", ("groups", "wide"), "rep", None),
            P("rep", None),
            P("rep", None),
            P("rep", None),
            P(None, "planes", None),
            P(),
            P(),
            P("wide", None, None),
            P("wide", None),
        ),
        out_specs=(
            P("planes", ("groups", "wide"), "rep"),
            P("planes", ("groups", "wide"), "rep", None),
        ),
        check_vma=False,
    )
```

```python
import jax
import jax.numpy as jnp
from jax import lax
from jax.experimental import pallas as pl
from jax.experimental.pallas import tpu as pltpu
from jax.sharding import PartitionSpec as P

MESH = pl.DeviceIdType.MESH
BF = jnp.bfloat16
F32 = jnp.float32
I32 = jnp.int32
LANES = 128
TILE = 16


def iota(shape, dim):
    return lax.broadcasted_iota(I32, shape, dim)


def from_taps(tap_ref, where_tap):
    weights = jnp.zeros(where_tap.shape, F32)
    for k in range(tap_ref.shape[0]):
        weights = jnp.where(where_tap == k, tap_ref[k], weights)
    return weights.astype(BF)


def whole_kernel(
    movie_hbm, temp_hbm, sup_hbm, mask_hbm, own_hbm, row_hbm, col_hbm, gain_hbm, dil_hbm,
    tr_out, resid, row_adj, col_adj,
    movie, temp_raw, sup_ref, mask_ref, own_ref, row_ref, col_ref, gain_ref, dil_ref, temp32, temp, temp_t, col_fwd, row_fwd, lag_own,
    smooth, fbuf, pall, part, xrecv, zsend, gath, lag_all, tbuf, tr_all, tr32, tt32, fold,
    in_s, h1_s, h1_r, h2_s, h2_r,
    lag_s, lag_r, x1_s, x1_r, z1_s, z1_r, z2_s, z2_r, x2_s, x2_r,
):
    np_ = lax.axis_size("planes")
    nw = lax.axis_size("wide")
    nr = lax.axis_size("rep")
    p = lax.axis_index("planes")
    z = lax.axis_index("wide")
    r = lax.axis_index("rep")
    planes, frames, rows, cols = movie.shape
    pixels = planes * cols
    blocks, hb, _, comps = part.shape
    shapes = temp.shape[0]
    total = nw * frames
    pad = (smooth.shape[1] - rows) // 2
    rim = (row_ref.shape[0] - 1) // 2
    col_rim = (col_ref.shape[0] - 1) // 2

    barrier = pltpu.get_barrier_semaphore()
    for k in range(1, nw):
        pl.semaphore_signal(barrier, inc=1, device_id={"wide": lax.rem(z + k, nw)}, device_id_type=MESH)
    for k in range(1, np_):
        pl.semaphore_signal(barrier, inc=1, device_id={"planes": lax.rem(p + k, np_)}, device_id_type=MESH)

    @pl.when(r > 0)
    def _():
        pl.semaphore_signal(barrier, inc=1, device_id={"rep": r - 1}, device_id_type=MESH)

    @pl.when(r < nr - 1)
    def _():
        pl.semaphore_signal(barrier, inc=1, device_id={"rep": r + 1}, device_id_type=MESH)

    col_in, movie_in, row_in, gain_in, dil_in, temp_in, mask_in, sup_in, own_in = [
        pltpu.make_async_copy(src, dst, in_s.at[n]) for n, (src, dst) in enumerate((
            (col_hbm, col_ref), (movie_hbm, movie), (row_hbm, row_ref), (gain_hbm, gain_ref), (dil_hbm, dil_ref),
            (temp_hbm, temp_raw), (mask_hbm, mask_ref), (sup_hbm, sup_ref), (own_hbm, own_ref)))]
    for copy in (col_in, movie_in, row_in, gain_in, dil_in, temp_in, mask_in, sup_in, own_in):
        copy.start()

    col_fwd[...] = jnp.zeros(col_fwd.shape, BF)
    col_adj[...] = jnp.zeros(col_adj.shape, BF)
    gap = iota((cols, cols), 0) - iota((cols, cols), 1)
    col_in.wait()
    fwd_block = from_taps(col_ref, gap + col_rim)
    for q in range(planes):
        side = slice(q * cols, (q + 1) * cols)
        col_fwd[side, side] = fwd_block

    zeros = jnp.zeros((frames, pad, pixels), BF)

    @pl.when(r == 0)
    def _():
        smooth[:, :pad, :] = zeros
        resid[:, :pad, :] = zeros

    @pl.when(r == nr - 1)
    def _():
        smooth[:, pad + rows :, :] = zeros
        resid[:, pad + rows :, :] = zeros

    movie_in.wait()
    step = max(1, min(frames, 512 // rows))
    for f in range(0, frames, step):
        x = jnp.concatenate([movie[q, f : f + step].reshape(step * rows, cols) for q in range(planes)], axis=1)
        y = jnp.dot(x, col_fwd[...], preferred_element_type=F32).astype(BF)
        smooth[f : f + step, pad : pad + rows, :] = y.reshape(step, rows, pixels)

    edge = iota((rows, rows + 2 * pad), 1) - iota((rows, rows + 2 * pad), 0) - pad
    row_in.wait()
    row_fwd[...] = from_taps(row_ref, edge + rim)

    gain_in.wait()
    dil_in.wait()
    taps_t = gain_ref.shape[2]
    wide_lags = 2 * total
    lag = iota((taps_t, wide_lags), 1) - (total - 1)
    offset = iota((taps_t, wide_lags), 0) - (taps_t - 1) // 2
    kern = jnp.zeros((1, wide_lags), F32)
    for b in range(gain_ref.shape[0]):
        hits = jnp.where(lag == dil_ref[b] * offset, 1.0, 0.0)
        kern = kern + jnp.dot(
            gain_ref[b], hits, precision=lax.Precision.HIGHEST, preferred_element_type=F32)
    kern = jnp.broadcast_to(kern, (TILE, wide_lags))
    for t in range(0, total, TILE):
        turned = pltpu.roll(kern, (total + 1 + t) % wide_lags, 1, stride=1, stride_axis=0)
        lag_own[t : t + TILE, :] = turned[:, :total].astype(BF)

    pl.semaphore_wait(
        barrier, nw - 1 + np_ - 1 + (r > 0).astype(I32) + (r < nr - 1).astype(I32))

    def halo_down(ext, send, recv):
        return pltpu.make_async_remote_copy(
            src_ref=ext.at[:, pl.ds(rows, pad), :], dst_ref=ext.at[:, pl.ds(0, pad), :],
            send_sem=send.at[0], recv_sem=recv.at[0],
            device_id={"rep": lax.rem(r + 1, nr)}, device_id_type=MESH)

    def halo_up(ext, send, recv):
        return pltpu.make_async_remote_copy(
            src_ref=ext.at[:, pl.ds(pad, pad), :], dst_ref=ext.at[:, pl.ds(rows + pad, pad), :],
            send_sem=send.at[1], recv_sem=recv.at[1],
            device_id={"rep": lax.rem(r + nr - 1, nr)}, device_id_type=MESH)

    def halo_start(ext, send, recv):
        @pl.when(r < nr - 1)
        def _():
            halo_down(ext, send, recv).start()

        @pl.when(r > 0)
        def _():
            halo_up(ext, send, recv).start()

    def halo_wait(ext, send, recv):
        @pl.when(r < nr - 1)
        def _():
            halo_down(ext, send, recv).wait_send()
            halo_up(ext, send, recv).wait_recv()

        @pl.when(r > 0)
        def _():
            halo_up(ext, send, recv).wait_send()
            halo_down(ext, send, recv).wait_recv()

    halo_start(smooth, h1_s, h1_r)

    def to_wide(src, dst, send, recv, k):
        return pltpu.make_async_remote_copy(
            src_ref=src, dst_ref=dst, send_sem=send.at[k - 1], recv_sem=recv.at[k - 1],
            device_id={"wide": lax.rem(z + k, nw)}, device_id_type=MESH)

    def to_plane(src, dst, send, recv, dp, zi):
        slot = (dp - 1) * nw + zi
        return pltpu.make_async_remote_copy(
            src_ref=src, dst_ref=dst, send_sem=send.at[slot], recv_sem=recv.at[slot],
            device_id={"planes": lax.rem(p + dp, np_)}, device_id_type=MESH)

    def lag_copy(k):
        return to_wide(lag_own, lag_all.at[z], lag_s, lag_r, k)

    def x1_copy(dp, zi):
        return to_plane(part.at[lax.rem(p + dp, np_) * nw + zi], xrecv.at[(dp - 1) * nw + zi], x1_s, x1_r, dp, zi)

    def z1_copy(k):
        return to_wide(zsend.at[lax.rem(z + k, nw)], gath.at[z], z1_s, z1_r, k)

    def z2_copy(k):
        return to_wide(tbuf.at[lax.rem(z + k, nw)], tr_all.at[p * nw + z], z2_s, z2_r, k)

    def x2_copy(dp, zi):
        return to_plane(tr_all.at[p * nw + zi], tr_all.at[p * nw + zi], x2_s, x2_r, dp, zi)

    for k in range(1, nw):
        lag_copy(k).start()
    lag_all[z] = lag_own[...]

    temp_in.wait()
    temp32[...] = temp_raw[...].astype(F32)
    for q in range(planes):
        side = slice(q * cols, (q + 1) * cols)
        one = temp32[pl.ds(q, shapes, stride=planes), :]
        temp[:, side] = one.astype(BF)
        temp_t[side, :] = jnp.transpose(one).astype(BF)

    for copy in (mask_in, sup_in, own_in):
        copy.wait()
    mask = mask_ref[...].astype(F32)
    halo_wait(smooth, h1_s, h1_r)
    for f in range(frames):
        along = jnp.dot(row_fwd[...], smooth[f], preferred_element_type=F32)
        for q in range(planes):
            one = along[:, q * cols : (q + 1) * cols] * mask
            fbuf[q, pl.ds(f, rows, stride=frames), :] = one.astype(BF).astype(F32)

    def project(b):
        base = pl.multiple_of(b * hb, hb)
        lines = pl.ds(pl.multiple_of(b * hb * frames, hb * frames), hb * frames)
        x = jnp.concatenate([fbuf[q, lines, :].astype(BF) for q in range(planes)], axis=1)
        pall[...] = jnp.dot(x, temp_t[...], preferred_element_type=F32)
        sup = sup_ref[pl.ds(base, hb), :]
        low = lax.rem(sup, LANES)
        high = lax.div(sup, LANES)
        for i in range(hb):
            lo = jnp.broadcast_to(low[i : i + 1, :], (frames, comps))
            hi = jnp.broadcast_to(high[i : i + 1, :], (frames, comps))
            got = jnp.zeros((frames, comps), F32)
            for q in range(shapes // LANES):
                piece = pall[i * frames : (i + 1) * frames, q * LANES : (q + 1) * LANES]
                picked = jnp.take_along_axis(piece, lo, axis=1, mode="promise_in_bounds")
                got = jnp.where(hi == q, picked, got)
            part[b, i] = got.astype(BF)

    def others(n, carry):
        dp = n // nw + 1
        zi = lax.rem(z + 1 + lax.rem(n, nw), nw)
        project(lax.rem(p + dp, np_) * nw + zi)
        x1_copy(dp, zi).start()
        return carry

    lax.fori_loop(0, (np_ - 1) * nw, others, 0)

    def mine(n, carry):
        zi = lax.rem(z + 1 + n, nw)
        b = p * nw + zi
        project(b)
        acc = part[b].astype(F32)
        for dp in range(1, np_):
            x1_copy(dp, zi).wait_recv()
            acc = acc + xrecv[(dp - 1) * nw + zi].astype(F32)
        zsend[zi] = acc.astype(BF)

        @pl.when(n < nw - 1)
        def _():
            z1_copy(n + 1).start()

        return carry

    lax.fori_loop(0, nw, mine, 0)
    gath[z] = zsend[z]

    row_adj[...] = from_taps(row_ref, rim - edge)
    adj_block = from_taps(col_ref, col_rim - gap)
    for q in range(planes):
        side = slice(q * cols, (q + 1) * cols)
        col_adj[side, side] = adj_block

    def arrived(k, carry):
        lag_copy(k).wait()
        z1_copy(k).wait()
        return carry

    lax.fori_loop(1, nw, arrived, 0)

    me = p * nw + z
    for i in range(hb):
        table = lag_all[own_ref[me * hb + i]]
        columns = gath[:, i].reshape(total, comps)
        scores = jnp.dot(table, columns, preferred_element_type=F32)
        tbuf[:, i] = jnp.maximum(scores, 0.0).astype(BF).reshape(nw, frames, comps)

    def give(k, carry):
        z2_copy(k).start()
        return carry

    lax.fori_loop(1, nw, give, 0)
    tr_all[me] = tbuf[z]

    tile = min(256, shapes)
    groups = tile // TILE
    ids = (iota((groups, TILE, comps), 0) * TILE + iota((groups, TILE, comps), 1)).astype(F32).astype(BF)

    def model(b):
        base = pl.multiple_of(b * hb, hb)
        first = pl.multiple_of(b * hb * frames, hb * frames)
        sup = sup_ref[pl.ds(base, hb), :]
        for i in range(hb):
            now = tr_all[b, i]
            tr32[pl.ds(first + i * frames, frames), :] = now.astype(F32)
            for q in range(0, shapes, tile):
                row = (sup[i : i + 1, :] - q).astype(F32)
                row = jnp.broadcast_to(row, (TILE, comps)).astype(BF)
                hot = jnp.where(ids == row[None], jnp.ones((), BF), jnp.zeros((), BF)).reshape(tile, comps)
                fold[i * frames : (i + 1) * frames, q : q + tile] = lax.dot_general(
                    now, hot, (((1,), (1,)), ((), ())), preferred_element_type=F32).astype(BF)
        out = jnp.dot(fold[...], temp[...], preferred_element_type=F32)
        lines = pl.ds(first, hb * frames)
        for q in range(planes):
            fbuf[q, lines, :] = fbuf[q, lines, :] - out[:, q * cols : (q + 1) * cols]

    def same_plane(k, carry):
        zi = lax.rem(z + nw - k, nw)

        @pl.when(k > 0)
        def _():
            z2_copy(lax.max(k, 1)).wait_recv()

        for dp in range(1, np_):
            x2_copy(dp, zi).start()
        model(p * nw + zi)
        return carry

    lax.fori_loop(0, nw, same_plane, 0)

    def other_planes(n, carry):
        dp = n // nw + 1
        zi = lax.rem(z + nw - lax.rem(n, nw), nw)
        x2_copy(dp, zi).wait_recv()
        model(lax.rem(p + np_ - dp, np_) * nw + zi)
        return carry

    lax.fori_loop(0, (np_ - 1) * nw, other_planes, 0)

    for f in range(frames):
        for q in range(planes):
            one = fbuf[q, pl.ds(f, rows, stride=frames), :] * mask
            resid[f, pad : pad + rows, q * cols : (q + 1) * cols] = one.astype(BF)
    halo_start(resid, h2_s, h2_r)

    share = tr_out.shape[0]
    chosen = iota((share, comps), 1) == iota((share, comps), 0) + p * share
    chosen = jnp.where(chosen, 1.0, 0.0).astype(BF)
    for f in range(frames):
        one = tr32[pl.ds(f, rows, stride=frames), :].astype(BF)
        tt32[pl.ds(f, share, stride=frames), :] = lax.dot_general(
            chosen, one, (((1,), (1,)), ((), ())), preferred_element_type=F32)
    tr_out[...] = tt32[...].astype(BF).reshape(share, frames, rows)

    halo_wait(resid, h2_s, h2_r)

    def drained_planes(n, carry):
        x1_copy(n // nw + 1, lax.rem(n, nw)).wait_send()
        x2_copy(n // nw + 1, lax.rem(n, nw)).wait_send()
        return carry

    lax.fori_loop(0, (np_ - 1) * nw, drained_planes, 0)

    def drained_wide(k, carry):
        z2_copy(k).wait_send()
        return carry

    lax.fori_loop(1, nw, drained_wide, 0)


def back_kernel(tr_ref, resid, row_adj, col_adj, tr_hbm, back_hbm, back_out, out_s):
    planes, frames, rows, cols = back_out.shape
    tr_copy = pltpu.make_async_copy(tr_ref, tr_hbm, out_s.at[0])
    tr_copy.start()
    step = max(1, frames // 4)
    copies = []
    for f0 in range(0, frames, step):
        for f in range(f0, f0 + step):
            y = jnp.dot(row_adj[...], resid[f], preferred_element_type=F32).astype(BF)
            y = jnp.dot(y, col_adj[...], preferred_element_type=F32).astype(BF)
            for q in range(planes):
                back_out[q, f] = y[:, q * cols : (q + 1) * cols]
        copy = pltpu.make_async_copy(
            back_out.at[:, pl.ds(f0, step)], back_hbm.at[:, pl.ds(f0, step)], out_s.at[1 + f0 // step])
        copy.start()
        copies.append(copy)
    tr_copy.wait()
    for copy in copies:
        copy.wait()


def on_device(
    movie_frames, pixel_mask, tile_owner, support, templates, row_taps, col_taps, lag_gains, dilations
):
    planes, frames, rows, cols = movie_frames.shape
    np_ = lax.axis_size("planes")
    nw = lax.axis_size("wide")
    blocks = np_ * nw
    hb = rows // blocks
    comps = support.shape[1]
    shapes = templates.shape[0]
    total = nw * frames
    pixels = planes * cols
    rim = (row_taps.shape[0] - 1) // 2
    pad = -(-rim // TILE) * TILE
    share = comps // np_
    piece = (hb, frames, comps)
    hbm = pl.BlockSpec(memory_space=pltpu.HBM)
    vm = pl.BlockSpec(memory_space=pltpu.VMEM)
    dma = pltpu.SemaphoreType.DMA
    middle = pl.pallas_call(
        whole_kernel,
        out_shape=(
            jax.ShapeDtypeStruct((share, frames, rows), BF),
            jax.ShapeDtypeStruct((frames, rows + 2 * pad, pixels), BF),
            jax.ShapeDtypeStruct((rows, rows + 2 * pad), BF),
            jax.ShapeDtypeStruct((pixels, pixels), BF),
        ),
        in_specs=[hbm] * 9,
        out_specs=(vm,) * 4,
        scratch_shapes=[
            pltpu.VMEM(movie_frames.shape, BF),
            pltpu.VMEM((shapes * planes, cols), BF),
            pltpu.VMEM(support.shape, I32),
            pltpu.VMEM(pixel_mask.shape, I32),
            pltpu.SMEM((rows,), I32),
            pltpu.SMEM(row_taps.shape, F32),
            pltpu.SMEM(col_taps.shape, F32),
            pltpu.VMEM((lag_gains.shape[1], 1, lag_gains.shape[2]), F32),
            pltpu.SMEM((dilations.shape[1],), I32),
            pltpu.VMEM((shapes * planes, cols), F32),
            pltpu.VMEM((shapes, pixels), BF),
            pltpu.VMEM((pixels, shapes), BF),
            pltpu.VMEM((pixels, pixels), BF),
            pltpu.VMEM((rows, rows + 2 * pad), BF),
            pltpu.VMEM((total, total), BF),
            pltpu.VMEM((frames, rows + 2 * pad, pixels), BF),
            pltpu.VMEM((planes, rows * frames, cols), F32),
            pltpu.VMEM((hb * frames, shapes), F32),
            pltpu.VMEM((blocks,) + piece, BF),
            pltpu.VMEM(((np_ - 1) * nw,) + piece, BF),
            pltpu.VMEM((nw,) + piece, BF),
            pltpu.VMEM((nw,) + piece, BF),
            pltpu.VMEM((nw, total, total), BF),
            pltpu.VMEM((nw,) + piece, BF),
            pltpu.VMEM((blocks,) + piece, BF),
            pltpu.VMEM((rows * frames, comps), F32),
            pltpu.VMEM((share * frames, rows), F32),
            pltpu.VMEM((hb * frames, shapes), BF),
            dma((9,)), dma((2,)), dma((2,)), dma((2,)), dma((2,)),
            dma((nw - 1,)), dma((nw - 1,)),
            dma(((np_ - 1) * nw,)), dma(((np_ - 1) * nw,)),
            dma((nw - 1,)), dma((nw - 1,)),
            dma((nw - 1,)), dma((nw - 1,)),
            dma(((np_ - 1) * nw,)), dma(((np_ - 1) * nw,)),
        ],
        compiler_params=pltpu.CompilerParams(
            collective_id=0, has_side_effects=True, vmem_limit_bytes=40 * 1024 * 1024
        ),
    )(*[pltpu.with_memory_space_constraint(x, pltpu.HBM) for x in (
        movie_frames, templates.reshape(shapes * planes, cols), support, pixel_mask, tile_owner[:, 0],
        row_taps, col_taps, jnp.transpose(lag_gains, (1, 0, 2)), dilations[0],
    )])
    return pl.pallas_call(
        back_kernel,
        out_shape=(
            jax.ShapeDtypeStruct((share, frames, rows), BF),
            jax.ShapeDtypeStruct(movie_frames.shape, BF),
        ),
        in_specs=[vm] * 4,
        out_specs=(hbm, hbm),
        scratch_shapes=[pltpu.VMEM(movie_frames.shape, BF), dma((5,))],
        compiler_params=pltpu.CompilerParams(vmem_limit_bytes=16 * 1024 * 1024),
    )(*middle)


def solution(mesh):
    return jax.shard_map(
        on_device,
        mesh=mesh,
        in_specs=(
            P("planes", ("groups", "wide"), "rep", None),
            P("rep", None),
            P("rep", None),
            P("rep", None),
            P(None, "planes", None),
            P(),
            P(),
            P("wide", None, None),
            P("wide", None),
        ),
        out_specs=(
            P("planes", ("groups", "wide"), "rep"),
            P("planes", ("groups", "wide"), "rep", None),
        ),
        check_vma=False,
    )
```

```python
import jax
import jax.numpy as jnp
from jax import lax
from jax.experimental import pallas as pl
from jax.experimental.pallas import tpu as pltpu
from jax.sharding import PartitionSpec as P

MESH = pl.DeviceIdType.MESH
BF = jnp.bfloat16
F32 = jnp.float32
I32 = jnp.int32
LANES = 128
TILE = 16


def iota(shape, dim):
    return lax.broadcasted_iota(I32, shape, dim)


def from_taps(tap_ref, where_tap):
    weights = jnp.zeros(where_tap.shape, F32)
    for k in range(tap_ref.shape[0]):
        weights = jnp.where(where_tap == k, tap_ref[k], weights)
    return weights.astype(BF)


def whole_kernel(
    movie_hbm, temp_hbm, sup_hbm, mask_hbm, own_hbm, row_hbm, col_hbm, gain_hbm, dil_hbm,
    tr_out, resid, row_adj, col_adj,
    movie, temp_raw, sup_ref, mask_ref, own_ref, row_ref, col_ref, gain_ref, dil_ref, temp32, temp, temp_t, col_fwd, row_fwd, lag_own,
    smooth, fbuf, pall, part, xrecv, zsend, gath, lag_all, tbuf, tr_all, tr32, tt32, fold,
    in_s, far_s, h1_s, h1_r, h2_s, h2_r,
    lag_s, lag_r, x1_s, x1_r, z1_s, z1_r, z2_s, z2_r, x2_s, x2_r,
):
    np_ = lax.axis_size("planes")
    nw = lax.axis_size("wide")
    nr = lax.axis_size("rep")
    p = lax.axis_index("planes")
    z = lax.axis_index("wide")
    r = lax.axis_index("rep")
    planes, frames, rows, cols = movie.shape
    pixels = planes * cols
    blocks, hb, _, comps = part.shape
    shapes = temp.shape[0]
    total = nw * frames
    pad = (smooth.shape[1] - rows) // 2
    rim = (row_ref.shape[0] - 1) // 2
    col_rim = (col_ref.shape[0] - 1) // 2

    barrier = pltpu.get_barrier_semaphore()
    for k in range(1, np_):
        pl.semaphore_signal(barrier, inc=1, device_id={"planes": lax.rem(p + k, np_)}, device_id_type=MESH)

    def greet(sem_low, sem_high, axis, at, count):
        @pl.when(at > 0)
        def _():
            pl.semaphore_signal(sem_low, inc=1, device_id={axis: at - 1}, device_id_type=MESH)

        @pl.when(at < count - 1)
        def _():
            pl.semaphore_signal(sem_high, inc=1, device_id={axis: at + 1}, device_id_type=MESH)

    greet(barrier, barrier, "rep", r, nr)
    greet(barrier, barrier, "wide", z, nw)

    col_in, movie_in, row_in, gain_in, dil_in, temp_in, mask_in, sup_in, own_in = [
        pltpu.make_async_copy(src, dst, in_s.at[n]) for n, (src, dst) in enumerate((
            (col_hbm, col_ref), (movie_hbm, movie), (row_hbm, row_ref), (gain_hbm, gain_ref), (dil_hbm, dil_ref),
            (temp_hbm, temp_raw), (mask_hbm, mask_ref), (sup_hbm, sup_ref), (own_hbm, own_ref)))]
    for copy in (col_in, movie_in, row_in, gain_in, dil_in, temp_in, mask_in, sup_in, own_in):
        copy.start()

    col_fwd[...] = jnp.zeros(col_fwd.shape, BF)
    col_adj[...] = jnp.zeros(col_adj.shape, BF)
    gap = iota((cols, cols), 0) - iota((cols, cols), 1)
    col_in.wait()
    fwd_block = from_taps(col_ref, gap + col_rim)
    for q in range(planes):
        side = slice(q * cols, (q + 1) * cols)
        col_fwd[side, side] = fwd_block

    zeros = jnp.zeros((frames, pad, pixels), BF)

    @pl.when(r == 0)
    def _():
        smooth[:, :pad, :] = zeros
        resid[:, :pad, :] = zeros

    @pl.when(r == nr - 1)
    def _():
        smooth[:, pad + rows :, :] = zeros
        resid[:, pad + rows :, :] = zeros

    movie_in.wait()
    step = max(1, min(frames, 512 // rows))
    for f in range(0, frames, step):
        x = jnp.concatenate([movie[q, f : f + step].reshape(step * rows, cols) for q in range(planes)], axis=1)
        y = jnp.dot(x, col_fwd[...], preferred_element_type=F32).astype(BF)
        smooth[f : f + step, pad : pad + rows, :] = y.reshape(step, rows, pixels)

    edge = iota((rows, rows + 2 * pad), 1) - iota((rows, rows + 2 * pad), 0) - pad
    row_in.wait()
    row_fwd[...] = from_taps(row_ref, edge + rim)

    gain_in.wait()
    dil_in.wait()
    taps_t = gain_ref.shape[2]
    wide_lags = 2 * total
    lag = iota((taps_t, wide_lags), 1) - (total - 1)
    offset = iota((taps_t, wide_lags), 0) - (taps_t - 1) // 2
    kern = jnp.zeros((1, wide_lags), F32)
    for b in range(gain_ref.shape[0]):
        hits = jnp.where(lag == dil_ref[b] * offset, 1.0, 0.0)
        kern = kern + jnp.dot(
            gain_ref[b], hits, precision=lax.Precision.HIGHEST, preferred_element_type=F32)
    kern = jnp.broadcast_to(kern, (TILE, wide_lags))
    for t in range(0, total, TILE):
        turned = pltpu.roll(kern, (total + 1 + t) % wide_lags, 1, stride=1, stride_axis=0)
        lag_own[t : t + TILE, :] = turned[:, :total].astype(BF)

    beside = sum((at > 0).astype(I32) + (at < count - 1).astype(I32) for at, count in ((r, nr), (z, nw)))
    pl.semaphore_wait(barrier, np_ - 1 + beside)

    def halo_down(ext, send, recv):
        return pltpu.make_async_remote_copy(
            src_ref=ext.at[:, pl.ds(rows, pad), :], dst_ref=ext.at[:, pl.ds(0, pad), :],
            send_sem=send.at[0], recv_sem=recv.at[0],
            device_id={"rep": lax.rem(r + 1, nr)}, device_id_type=MESH)

    def halo_up(ext, send, recv):
        return pltpu.make_async_remote_copy(
            src_ref=ext.at[:, pl.ds(pad, pad), :], dst_ref=ext.at[:, pl.ds(rows + pad, pad), :],
            send_sem=send.at[1], recv_sem=recv.at[1],
            device_id={"rep": lax.rem(r + nr - 1, nr)}, device_id_type=MESH)

    def halo_start(ext, send, recv):
        @pl.when(r < nr - 1)
        def _():
            halo_down(ext, send, recv).start()

        @pl.when(r > 0)
        def _():
            halo_up(ext, send, recv).start()

    def halo_wait(ext, send, recv):
        @pl.when(r < nr - 1)
        def _():
            halo_down(ext, send, recv).wait_send()
            halo_up(ext, send, recv).wait_recv()

        @pl.when(r > 0)
        def _():
            halo_up(ext, send, recv).wait_send()
            halo_down(ext, send, recv).wait_recv()

    halo_start(smooth, h1_s, h1_r)

    def vouch(d):
        greet(far_s.at[1, d], far_s.at[0, d], "wide", z, nw)

    def vouched(d):
        @pl.when(z > 0)
        def _():
            pl.semaphore_wait(far_s.at[0, d], 1)

        @pl.when(z < nw - 1)
        def _():
            pl.semaphore_wait(far_s.at[1, d], 1)

    rounds = nw - 2
    if rounds > 0:
        vouch(0)

    paired = nw & (nw - 1) == 0

    def peer(k, sign=1):
        if not paired:
            return lax.rem(z + nw + sign * k, nw)
        found, bit = 0, 1
        while bit < nw:
            found = found + bit * lax.rem(lax.div(z, bit) + lax.div(k, bit), 2)
            bit *= 2
        return found

    def to_wide(src, dst, send, recv, k, slot):
        return pltpu.make_async_remote_copy(
            src_ref=src, dst_ref=dst, send_sem=send.at[slot], recv_sem=recv.at[slot],
            device_id={"wide": peer(k)}, device_id_type=MESH)

    def to_plane(src, dst, send, recv, dp, slot):
        return pltpu.make_async_remote_copy(
            src_ref=src, dst_ref=dst, send_sem=send.at[slot], recv_sem=recv.at[slot],
            device_id={"planes": lax.rem(p + dp, np_)}, device_id_type=MESH)

    groups = x1_s.shape[0] // ((np_ - 1) * nw)
    hg = hb // groups

    def some(g):
        return pl.ds(g * hg, hg)

    def lag_copy(k):
        return to_wide(lag_own, lag_all.at[z], lag_s, lag_r, k, k - 1)

    def x1_copy(dp, zi, g):
        slot = (dp - 1) * nw + zi
        return to_plane(
            part.at[lax.rem(p + dp, np_) * nw + zi, some(g)], xrecv.at[slot, some(g)],
            x1_s, x1_r, dp, slot * groups + g)

    def z1_copy(k, g):
        return to_wide(zsend.at[peer(k), some(g)], gath.at[z, some(g)], z1_s, z1_r, k, (k - 1) * groups + g)

    def z2_copy(k, g):
        return to_wide(
            tbuf.at[peer(k), some(g)], tr_all.at[p * nw + z, some(g)], z2_s, z2_r, k, (k - 1) * groups + g)

    def x2_copy(dp, zi, g):
        ours = tr_all.at[p * nw + zi, some(g)]
        return to_plane(ours, ours, x2_s, x2_r, dp, ((dp - 1) * nw + zi) * groups + g)

    temp_in.wait()
    temp32[...] = temp_raw[...].astype(F32)
    for q in range(planes):
        side = slice(q * cols, (q + 1) * cols)
        one = temp32[pl.ds(q, shapes, stride=planes), :]
        temp[:, side] = one.astype(BF)
        temp_t[side, :] = jnp.transpose(one).astype(BF)

    for copy in (mask_in, sup_in, own_in):
        copy.wait()
    mask = mask_ref[...].astype(F32)
    halo_wait(smooth, h1_s, h1_r)
    if rounds > 0:
        vouched(0)
    if rounds > 1:
        vouch(1)
    for f in range(frames):
        along = jnp.dot(row_fwd[...], smooth[f], preferred_element_type=F32)
        for q in range(planes):
            one = along[:, q * cols : (q + 1) * cols] * mask
            fbuf[q, pl.ds(f, rows, stride=frames), :] = one.astype(BF).astype(F32)

    def project(b, g):
        base = pl.multiple_of(b * hb + g * hg, hg)
        lines = pl.ds(pl.multiple_of((b * hb + g * hg) * frames, hg * frames), hg * frames)
        x = jnp.concatenate([fbuf[q, lines, :].astype(BF) for q in range(planes)], axis=1)
        pall[...] = jnp.dot(x, temp_t[...], preferred_element_type=F32)
        sup = sup_ref[pl.ds(base, hg), :]
        low = lax.rem(sup, LANES)
        high = lax.div(sup, LANES)
        for i in range(hg):
            lo = jnp.broadcast_to(low[i : i + 1, :], (frames, comps))
            hi = jnp.broadcast_to(high[i : i + 1, :], (frames, comps))
            got = jnp.zeros((frames, comps), F32)
            for q in range(shapes // LANES):
                piece = pall[i * frames : (i + 1) * frames, q * LANES : (q + 1) * LANES]
                picked = jnp.take_along_axis(piece, lo, axis=1, mode="promise_in_bounds")
                got = jnp.where(hi == q, picked, got)
            part[b, g * hg + i] = got.astype(BF)

    def others(n, carry):
        g = lax.div(n, (np_ - 1) * nw)
        dp = lax.rem(lax.div(n, nw), np_ - 1) + 1
        zi = peer(nw - 1 - lax.rem(n, nw))
        project(lax.rem(p + dp, np_) * nw + zi, g)
        x1_copy(dp, zi, g).start()
        return carry

    lax.fori_loop(0, groups * (np_ - 1) * nw, others, 0)

    for d in range(1, rounds):
        vouched(d)
        if d + 1 < rounds:
            vouch(d + 1)
    for k in range(1, nw):
        lag_copy(k).start()
    lag_all[z] = lag_own[...]

    def mine(n, carry):
        g = lax.div(n, nw)
        k = nw - 1 - lax.rem(n, nw)
        zi = peer(k)
        b = p * nw + zi
        project(b, g)
        acc = part[b, some(g)].astype(F32)
        for dp in range(1, np_):
            x1_copy(dp, zi, g).wait_recv()
            acc = acc + xrecv[(dp - 1) * nw + zi, some(g)].astype(F32)
        zsend[zi, some(g)] = acc.astype(BF)

        @pl.when(k > 0)
        def _():
            z1_copy(lax.max(k, 1), g).start()

        return carry

    lax.fori_loop(0, groups * nw, mine, 0)
    gath[z] = zsend[z]

    row_adj[...] = from_taps(row_ref, rim - edge)
    adj_block = from_taps(col_ref, col_rim - gap)
    for q in range(planes):
        side = slice(q * cols, (q + 1) * cols)
        col_adj[side, side] = adj_block

    def tables(k, carry):
        lag_copy(k).wait()
        return carry

    lax.fori_loop(1, nw, tables, 0)

    def second(n):
        return jnp.where(n < 2, n, nw + 1 - n)

    me = p * nw + z
    for g in range(groups):
        def arrived(k, carry):
            z1_copy(k, g).wait()
            return carry

        lax.fori_loop(1, nw, arrived, 0)
        for i in range(g * hg, (g + 1) * hg):
            table = lag_all[own_ref[me * hb + i]]
            columns = gath[:, i].reshape(total, comps)
            scores = jnp.dot(table, columns, preferred_element_type=F32)
            tbuf[:, i] = jnp.maximum(scores, 0.0).astype(BF).reshape(nw, frames, comps)

        def give(n, carry):
            z2_copy(second(n), g).start()
            return carry

        lax.fori_loop(1, nw, give, 0)
        tr_all[me, some(g)] = tbuf[z, some(g)]
        for dp in range(1, np_):
            x2_copy(dp, z, g).start()

    tile = min(256, shapes)
    ids = iota((tile // TILE, TILE, comps), 0) * TILE + iota((tile // TILE, TILE, comps), 1)
    ids = ids.astype(F32).astype(BF)

    def model(b, g):
        base = pl.multiple_of(b * hb + g * hg, hg)
        first = pl.multiple_of((b * hb + g * hg) * frames, hg * frames)
        sup = sup_ref[pl.ds(base, hg), :]
        for i in range(hg):
            now = tr_all[b, g * hg + i]
            tr32[pl.ds(first + i * frames, frames), :] = now.astype(F32)
            for q in range(0, shapes, tile):
                row = (sup[i : i + 1, :] - q).astype(F32)
                row = jnp.broadcast_to(row, (TILE, comps)).astype(BF)
                hot = jnp.where(ids == row[None], jnp.ones((), BF), jnp.zeros((), BF)).reshape(tile, comps)
                fold[i * frames : (i + 1) * frames, q : q + tile] = lax.dot_general(
                    now, hot, (((1,), (1,)), ((), ())), preferred_element_type=F32).astype(BF)
        out = jnp.dot(fold[...], temp[...], preferred_element_type=F32)
        lines = pl.ds(first, hg * frames)
        for q in range(planes):
            fbuf[q, lines, :] = fbuf[q, lines, :] - out[:, q * cols : (q + 1) * cols]

    def same_plane(n, carry):
        g = lax.div(n, nw)
        k = second(lax.rem(n, nw))
        zi = peer(k, -1)

        @pl.when(k > 0)
        def _():
            z2_copy(lax.max(k, 1), g).wait_recv()
            for dp in range(1, np_):
                x2_copy(dp, zi, g).start()

        model(p * nw + zi, g)
        return carry

    lax.fori_loop(0, groups * nw, same_plane, 0)

    def other_planes(n, carry):
        g = lax.div(n, (np_ - 1) * nw)
        dp = lax.rem(lax.div(n, nw), np_ - 1) + 1
        zi = peer(second(lax.rem(n, nw)), -1)
        x2_copy(dp, zi, g).wait_recv()
        model(lax.rem(p + np_ - dp, np_) * nw + zi, g)
        return carry

    lax.fori_loop(0, groups * (np_ - 1) * nw, other_planes, 0)

    for f in range(frames):
        for q in range(planes):
            one = fbuf[q, pl.ds(f, rows, stride=frames), :] * mask
            resid[f, pad : pad + rows, q * cols : (q + 1) * cols] = one.astype(BF)
    halo_start(resid, h2_s, h2_r)

    share = tr_out.shape[0]
    chosen = iota((share, comps), 1) == iota((share, comps), 0) + p * share
    chosen = jnp.where(chosen, 1.0, 0.0).astype(BF)
    for f in range(frames):
        one = tr32[pl.ds(f, rows, stride=frames), :].astype(BF)
        tt32[pl.ds(f, share, stride=frames), :] = lax.dot_general(
            chosen, one, (((1,), (1,)), ((), ())), preferred_element_type=F32)
    tr_out[...] = tt32[...].astype(BF).reshape(share, frames, rows)

    halo_wait(resid, h2_s, h2_r)

    def drained_planes(n, carry):
        dp, zi, g = lax.div(n, nw * groups) + 1, lax.rem(lax.div(n, groups), nw), lax.rem(n, groups)
        x1_copy(dp, zi, g).wait_send()
        x2_copy(dp, zi, g).wait_send()
        return carry

    lax.fori_loop(0, (np_ - 1) * nw * groups, drained_planes, 0)

    def drained_wide(n, carry):
        z2_copy(lax.div(n, groups) + 1, lax.rem(n, groups)).wait_send()
        return carry

    lax.fori_loop(0, (nw - 1) * groups, drained_wide, 0)


def back_kernel(tr_ref, resid, row_adj, col_adj, tr_hbm, back_hbm, back_out, out_s):
    planes, frames, rows, cols = back_out.shape
    tr_copy = pltpu.make_async_copy(tr_ref, tr_hbm, out_s.at[0])
    tr_copy.start()
    step = max(1, frames // 4)
    copies = []
    for f0 in range(0, frames, step):
        for f in range(f0, f0 + step):
            y = jnp.dot(row_adj[...], resid[f], preferred_element_type=F32).astype(BF)
            y = jnp.dot(y, col_adj[...], preferred_element_type=F32).astype(BF)
            for q in range(planes):
                back_out[q, f] = y[:, q * cols : (q + 1) * cols]
        copy = pltpu.make_async_copy(
            back_out.at[:, pl.ds(f0, step)], back_hbm.at[:, pl.ds(f0, step)], out_s.at[1 + f0 // step])
        copy.start()
        copies.append(copy)
    tr_copy.wait()
    for copy in copies:
        copy.wait()


def on_device(
    movie_frames, pixel_mask, tile_owner, support, templates, row_taps, col_taps, lag_gains, dilations
):
    planes, frames, rows, cols = movie_frames.shape
    np_ = lax.axis_size("planes")
    nw = lax.axis_size("wide")
    blocks = np_ * nw
    hb = rows // blocks
    groups = 2 if hb % 2 == 0 else 1
    comps = support.shape[1]
    shapes = templates.shape[0]
    total = nw * frames
    pixels = planes * cols
    rim = (row_taps.shape[0] - 1) // 2
    pad = -(-rim // TILE) * TILE
    share = comps // np_
    piece = (hb, frames, comps)
    hbm = pl.BlockSpec(memory_space=pltpu.HBM)
    vm = pl.BlockSpec(memory_space=pltpu.VMEM)
    dma = pltpu.SemaphoreType.DMA
    middle = pl.pallas_call(
        whole_kernel,
        out_shape=(
            jax.ShapeDtypeStruct((share, frames, rows), BF),
            jax.ShapeDtypeStruct((frames, rows + 2 * pad, pixels), BF),
            jax.ShapeDtypeStruct((rows, rows + 2 * pad), BF),
            jax.ShapeDtypeStruct((pixels, pixels), BF),
        ),
        in_specs=[hbm] * 9,
        out_specs=(vm,) * 4,
        scratch_shapes=[
            pltpu.VMEM(movie_frames.shape, BF),
            pltpu.VMEM((shapes * planes, cols), BF),
            pltpu.VMEM(support.shape, I32),
            pltpu.VMEM(pixel_mask.shape, I32),
            pltpu.SMEM((rows,), I32),
            pltpu.SMEM(row_taps.shape, F32),
            pltpu.SMEM(col_taps.shape, F32),
            pltpu.VMEM((lag_gains.shape[1], 1, lag_gains.shape[2]), F32),
            pltpu.SMEM((dilations.shape[1],), I32),
            pltpu.VMEM((shapes * planes, cols), F32),
            pltpu.VMEM((shapes, pixels), BF),
            pltpu.VMEM((pixels, shapes), BF),
            pltpu.VMEM((pixels, pixels), BF),
            pltpu.VMEM((rows, rows + 2 * pad), BF),
            pltpu.VMEM((total, total), BF),
            pltpu.VMEM((frames, rows + 2 * pad, pixels), BF),
            pltpu.VMEM((planes, rows * frames, cols), F32),
            pltpu.VMEM((hb // groups * frames, shapes), F32),
            pltpu.VMEM((blocks,) + piece, BF),
            pltpu.VMEM(((np_ - 1) * nw,) + piece, BF),
            pltpu.VMEM((nw,) + piece, BF),
            pltpu.VMEM((nw,) + piece, BF),
            pltpu.VMEM((nw, total, total), BF),
            pltpu.VMEM((nw,) + piece, BF),
            pltpu.VMEM((blocks,) + piece, BF),
            pltpu.VMEM((rows * frames, comps), F32),
            pltpu.VMEM((share * frames, rows), F32),
            pltpu.VMEM((hb // groups * frames, shapes), BF),
            dma((9,)), pltpu.SemaphoreType.REGULAR((2, max(1, nw - 2))), dma((2,)), dma((2,)), dma((2,)), dma((2,)),
            dma((nw - 1,)), dma((nw - 1,)),
            dma(((np_ - 1) * nw * groups,)), dma(((np_ - 1) * nw * groups,)),
            dma(((nw - 1) * groups,)), dma(((nw - 1) * groups,)),
            dma(((nw - 1) * groups,)), dma(((nw - 1) * groups,)),
            dma(((np_ - 1) * nw * groups,)), dma(((np_ - 1) * nw * groups,)),
        ],
        compiler_params=pltpu.CompilerParams(
            collective_id=0, has_side_effects=True, vmem_limit_bytes=40 * 1024 * 1024
        ),
    )(*[pltpu.with_memory_space_constraint(x, pltpu.HBM) for x in (
        movie_frames, templates.reshape(shapes * planes, cols), support, pixel_mask, tile_owner[:, 0],
        row_taps, col_taps, jnp.transpose(lag_gains, (1, 0, 2)), dilations[0],
    )])
    return pl.pallas_call(
        back_kernel,
        out_shape=(
            jax.ShapeDtypeStruct((share, frames, rows), BF),
            jax.ShapeDtypeStruct(movie_frames.shape, BF),
        ),
        in_specs=[vm] * 4,
        out_specs=(hbm, hbm),
        scratch_shapes=[pltpu.VMEM(movie_frames.shape, BF), dma((5,))],
        compiler_params=pltpu.CompilerParams(vmem_limit_bytes=16 * 1024 * 1024),
    )(*middle)


def solution(mesh):
    return jax.shard_map(
        on_device,
        mesh=mesh,
        in_specs=(
            P("planes", ("groups", "wide"), "rep", None),
            P("rep", None),
            P("rep", None),
            P("rep", None),
            P(None, "planes", None),
            P(),
            P(),
            P("wide", None, None),
            P("wide", None),
        ),
        out_specs=(
            P("planes", ("groups", "wide"), "rep"),
            P("planes", ("groups", "wide"), "rep", None),
        ),
        check_vma=False,
    )
```

```python
import jax
import jax.numpy as jnp
from jax import lax
from jax.experimental import pallas as pl
from jax.experimental.pallas import tpu as pltpu
from jax.sharding import PartitionSpec as P

MESH = pl.DeviceIdType.MESH
BF = jnp.bfloat16
F32 = jnp.float32
I32 = jnp.int32
LANES = 128
TILE = 16


def iota(shape, dim):
    return lax.broadcasted_iota(I32, shape, dim)


def from_taps(tap_ref, where_tap):
    weights = jnp.zeros(where_tap.shape, F32)
    for k in range(tap_ref.shape[0]):
        weights = jnp.where(where_tap == k, tap_ref[k], weights)
    return weights.astype(BF)


def whole_kernel(
    movie_hbm, temp_hbm, sup_hbm, mask_hbm, own_hbm, row_hbm, col_hbm, gain_hbm, dil_hbm,
    tr_out, resid, row_adj, col_adj,
    movie, temp_raw, sup_ref, mask_ref, own_ref, row_ref, col_ref, gain_ref, dil_ref, temp32, temp, temp_t, col_fwd, row_fwd, lag_own,
    smooth, fbuf, pall, part, xrecv, zsend, gath, lag_all, tbuf, tr_all, tr32, tt32, fold,
    in_s, far_s, h1_s, h1_r, h2_s, h2_r,
    lag_s, lag_r, x1_s, x1_r, z1_s, z1_r, z2_s, z2_r, x2_s, x2_r,
):
    np_ = lax.axis_size("planes")
    nw = lax.axis_size("wide")
    nr = lax.axis_size("rep")
    p = lax.axis_index("planes")
    z = lax.axis_index("wide")
    r = lax.axis_index("rep")
    planes, frames, rows, cols = movie.shape
    pixels = planes * cols
    blocks, hb, _, comps = part.shape
    shapes = temp.shape[0]
    total = nw * frames
    pad = (smooth.shape[1] - rows) // 2
    rim = (row_ref.shape[0] - 1) // 2
    col_rim = (col_ref.shape[0] - 1) // 2

    barrier = pltpu.get_barrier_semaphore()
    for k in range(1, np_):
        pl.semaphore_signal(barrier, inc=1, device_id={"planes": lax.rem(p + k, np_)}, device_id_type=MESH)

    def greet(sem_low, sem_high, axis, at, count):
        @pl.when(at > 0)
        def _():
            pl.semaphore_signal(sem_low, inc=1, device_id={axis: at - 1}, device_id_type=MESH)

        @pl.when(at < count - 1)
        def _():
            pl.semaphore_signal(sem_high, inc=1, device_id={axis: at + 1}, device_id_type=MESH)

    greet(barrier, barrier, "rep", r, nr)
    greet(barrier, barrier, "wide", z, nw)

    col_in, movie_in, row_in, gain_in, dil_in, temp_in, mask_in, sup_in, own_in = [
        pltpu.make_async_copy(src, dst, in_s.at[n]) for n, (src, dst) in enumerate((
            (col_hbm, col_ref), (movie_hbm, movie), (row_hbm, row_ref), (gain_hbm, gain_ref), (dil_hbm, dil_ref),
            (temp_hbm, temp_raw), (mask_hbm, mask_ref), (sup_hbm, sup_ref), (own_hbm, own_ref)))]
    for copy in (col_in, movie_in, row_in, gain_in, dil_in, temp_in, mask_in, sup_in, own_in):
        copy.start()

    col_fwd[...] = jnp.zeros(col_fwd.shape, BF)
    col_adj[...] = jnp.zeros(col_adj.shape, BF)
    gap = iota((cols, cols), 0) - iota((cols, cols), 1)
    col_in.wait()
    fwd_block = from_taps(col_ref, gap + col_rim)
    for q in range(planes):
        side = slice(q * cols, (q + 1) * cols)
        col_fwd[side, side] = fwd_block

    zeros = jnp.zeros((frames, pad, pixels), BF)

    @pl.when(r == 0)
    def _():
        smooth[:, :pad, :] = zeros
        resid[:, :pad, :] = zeros

    @pl.when(r == nr - 1)
    def _():
        smooth[:, pad + rows :, :] = zeros
        resid[:, pad + rows :, :] = zeros

    movie_in.wait()
    step = max(1, min(frames, 512 // rows))
    for f in range(0, frames, step):
        x = jnp.concatenate([movie[q, f : f + step].reshape(step * rows, cols) for q in range(planes)], axis=1)
        y = jnp.dot(x, col_fwd[...], preferred_element_type=F32).astype(BF)
        smooth[f : f + step, pad : pad + rows, :] = y.reshape(step, rows, pixels)

    edge = iota((rows, rows + 2 * pad), 1) - iota((rows, rows + 2 * pad), 0) - pad
    row_in.wait()
    row_fwd[...] = from_taps(row_ref, edge + rim)

    gain_in.wait()
    dil_in.wait()
    taps_t = gain_ref.shape[2]
    wide_lags = 2 * total
    lag = iota((taps_t, wide_lags), 1) - (total - 1)
    offset = iota((taps_t, wide_lags), 0) - (taps_t - 1) // 2
    kern = jnp.zeros((1, wide_lags), F32)
    for b in range(gain_ref.shape[0]):
        hits = jnp.where(lag == dil_ref[b] * offset, 1.0, 0.0)
        kern = kern + jnp.dot(
            gain_ref[b], hits, precision=lax.Precision.HIGHEST, preferred_element_type=F32)
    kern = jnp.broadcast_to(kern, (TILE, wide_lags))
    for t in range(0, total, TILE):
        turned = pltpu.roll(kern, (total + 1 + t) % wide_lags, 1, stride=1, stride_axis=0)
        lag_own[t : t + TILE, :] = turned[:, :total].astype(BF)

    beside = sum((at > 0).astype(I32) + (at < count - 1).astype(I32) for at, count in ((r, nr), (z, nw)))
    pl.semaphore_wait(barrier, np_ - 1 + beside)

    def halo_down(ext, send, recv):
        return pltpu.make_async_remote_copy(
            src_ref=ext.at[:, pl.ds(rows, pad), :], dst_ref=ext.at[:, pl.ds(0, pad), :],
            send_sem=send.at[0], recv_sem=recv.at[0],
            device_id={"rep": lax.rem(r + 1, nr)}, device_id_type=MESH)

    def halo_up(ext, send, recv):
        return pltpu.make_async_remote_copy(
            src_ref=ext.at[:, pl.ds(pad, pad), :], dst_ref=ext.at[:, pl.ds(rows + pad, pad), :],
            send_sem=send.at[1], recv_sem=recv.at[1],
            device_id={"rep": lax.rem(r + nr - 1, nr)}, device_id_type=MESH)

    def halo_start(ext, send, recv):
        @pl.when(r < nr - 1)
        def _():
            halo_down(ext, send, recv).start()

        @pl.when(r > 0)
        def _():
            halo_up(ext, send, recv).start()

    def halo_wait(ext, send, recv):
        @pl.when(r < nr - 1)
        def _():
            halo_down(ext, send, recv).wait_send()
            halo_up(ext, send, recv).wait_recv()

        @pl.when(r > 0)
        def _():
            halo_up(ext, send, recv).wait_send()
            halo_down(ext, send, recv).wait_recv()

    halo_start(smooth, h1_s, h1_r)

    def vouch(d):
        greet(far_s.at[1, d], far_s.at[0, d], "wide", z, nw)

    def vouched(d):
        @pl.when(z > 0)
        def _():
            pl.semaphore_wait(far_s.at[0, d], 1)

        @pl.when(z < nw - 1)
        def _():
            pl.semaphore_wait(far_s.at[1, d], 1)

    rounds = nw - 2
    if rounds > 0:
        vouch(0)

    paired = False

    def peer(k, sign=1):
        if not paired:
            return lax.rem(z + nw + sign * k, nw)
        found, bit = 0, 1
        while bit < nw:
            found = found + bit * lax.rem(lax.div(z, bit) + lax.div(k, bit), 2)
            bit *= 2
        return found

    def to_wide(src, dst, send, recv, k, slot):
        return pltpu.make_async_remote_copy(
            src_ref=src, dst_ref=dst, send_sem=send.at[slot], recv_sem=recv.at[slot],
            device_id={"wide": peer(k)}, device_id_type=MESH)

    def to_plane(src, dst, send, recv, dp, slot):
        return pltpu.make_async_remote_copy(
            src_ref=src, dst_ref=dst, send_sem=send.at[slot], recv_sem=recv.at[slot],
            device_id={"planes": lax.rem(p + dp, np_)}, device_id_type=MESH)

    groups = x1_s.shape[0] // ((np_ - 1) * nw)
    hg = hb // groups

    def some(g):
        return pl.ds(g * hg, hg)

    def lag_copy(k):
        return to_wide(lag_own, lag_all.at[z], lag_s, lag_r, k, k - 1)

    def x1_copy(dp, zi, g):
        slot = (dp - 1) * nw + zi
        return to_plane(
            part.at[lax.rem(p + dp, np_) * nw + zi, some(g)], xrecv.at[slot, some(g)],
            x1_s, x1_r, dp, slot * groups + g)

    def z1_copy(k, g):
        return to_wide(zsend.at[peer(k), some(g)], gath.at[z, some(g)], z1_s, z1_r, k, (k - 1) * groups + g)

    def z2_copy(k, g):
        return to_wide(
            tbuf.at[peer(k), some(g)], tr_all.at[p * nw + z, some(g)], z2_s, z2_r, k, (k - 1) * groups + g)

    def x2_copy(dp, zi, g):
        ours = tr_all.at[p * nw + zi, some(g)]
        return to_plane(ours, ours, x2_s, x2_r, dp, ((dp - 1) * nw + zi) * groups + g)

    temp_in.wait()
    temp32[...] = temp_raw[...].astype(F32)
    for q in range(planes):
        side = slice(q * cols, (q + 1) * cols)
        one = temp32[pl.ds(q, shapes, stride=planes), :]
        temp[:, side] = one.astype(BF)
        temp_t[side, :] = jnp.transpose(one).astype(BF)

    for copy in (mask_in, sup_in, own_in):
        copy.wait()
    mask = mask_ref[...].astype(F32)
    halo_wait(smooth, h1_s, h1_r)
    if rounds > 0:
        vouched(0)
    if rounds > 1:
        vouch(1)
    for f in range(frames):
        along = jnp.dot(row_fwd[...], smooth[f], preferred_element_type=F32)
        for q in range(planes):
            one = along[:, q * cols : (q + 1) * cols] * mask
            fbuf[q, pl.ds(f, rows, stride=frames), :] = one.astype(BF).astype(F32)

    def project(b, g):
        base = pl.multiple_of(b * hb + g * hg, hg)
        lines = pl.ds(pl.multiple_of((b * hb + g * hg) * frames, hg * frames), hg * frames)
        x = jnp.concatenate([fbuf[q, lines, :].astype(BF) for q in range(planes)], axis=1)
        pall[...] = jnp.dot(x, temp_t[...], preferred_element_type=F32)
        sup = sup_ref[pl.ds(base, hg), :]
        low = lax.rem(sup, LANES)
        high = lax.div(sup, LANES)
        for i in range(hg):
            lo = jnp.broadcast_to(low[i : i + 1, :], (frames, comps))
            hi = jnp.broadcast_to(high[i : i + 1, :], (frames, comps))
            got = jnp.zeros((frames, comps), F32)
            for q in range(shapes // LANES):
                piece = pall[i * frames : (i + 1) * frames, q * LANES : (q + 1) * LANES]
                picked = jnp.take_along_axis(piece, lo, axis=1, mode="promise_in_bounds")
                got = jnp.where(hi == q, picked, got)
            part[b, g * hg + i] = got.astype(BF)

    def others(n, carry):
        g = lax.div(n, (np_ - 1) * nw)
        dp = lax.rem(lax.div(n, nw), np_ - 1) + 1
        zi = peer(nw - 1 - lax.rem(n, nw))
        project(lax.rem(p + dp, np_) * nw + zi, g)
        x1_copy(dp, zi, g).start()
        return carry

    lax.fori_loop(0, groups * (np_ - 1) * nw, others, 0)

    for d in range(1, rounds):
        vouched(d)
        if d + 1 < rounds:
            vouch(d + 1)
    for k in range(1, nw):
        lag_copy(k).start()
    lag_all[z] = lag_own[...]

    def mine(n, carry):
        g = lax.div(n, nw)
        k = nw - 1 - lax.rem(n, nw)
        zi = peer(k)
        b = p * nw + zi
        project(b, g)
        acc = part[b, some(g)].astype(F32)
        for dp in range(1, np_):
            x1_copy(dp, zi, g).wait_recv()
            acc = acc + xrecv[(dp - 1) * nw + zi, some(g)].astype(F32)
        zsend[zi, some(g)] = acc.astype(BF)

        @pl.when(k > 0)
        def _():
            z1_copy(lax.max(k, 1), g).start()

        return carry

    lax.fori_loop(0, groups * nw, mine, 0)
    gath[z] = zsend[z]

    row_adj[...] = from_taps(row_ref, rim - edge)
    adj_block = from_taps(col_ref, col_rim - gap)
    for q in range(planes):
        side = slice(q * cols, (q + 1) * cols)
        col_adj[side, side] = adj_block

    def tables(k, carry):
        lag_copy(k).wait()
        return carry

    lax.fori_loop(1, nw, tables, 0)

    def second(n):
        return jnp.where(n < 2, n, nw + 1 - n)

    me = p * nw + z
    for g in range(groups):
        def arrived(k, carry):
            z1_copy(k, g).wait()
            return carry

        lax.fori_loop(1, nw, arrived, 0)
        for i in range(g * hg, (g + 1) * hg):
            table = lag_all[own_ref[me * hb + i]]
            columns = gath[:, i].reshape(total, comps)
            scores = jnp.dot(table, columns, preferred_element_type=F32)
            tbuf[:, i] = jnp.maximum(scores, 0.0).astype(BF).reshape(nw, frames, comps)

        def give(n, carry):
            z2_copy(second(n), g).start()
            return carry

        lax.fori_loop(1, nw, give, 0)
        tr_all[me, some(g)] = tbuf[z, some(g)]
        for dp in range(1, np_):
            x2_copy(dp, z, g).start()

    tile = min(256, shapes)
    ids = iota((tile // TILE, TILE, comps), 0) * TILE + iota((tile // TILE, TILE, comps), 1)
    ids = ids.astype(F32).astype(BF)

    def model(b, g):
        base = pl.multiple_of(b * hb + g * hg, hg)
        first = pl.multiple_of((b * hb + g * hg) * frames, hg * frames)
        sup = sup_ref[pl.ds(base, hg), :]
        for i in range(hg):
            now = tr_all[b, g * hg + i]
            tr32[pl.ds(first + i * frames, frames), :] = now.astype(F32)
            for q in range(0, shapes, tile):
                row = (sup[i : i + 1, :] - q).astype(F32)
                row = jnp.broadcast_to(row, (TILE, comps)).astype(BF)
                hot = jnp.where(ids == row[None], jnp.ones((), BF), jnp.zeros((), BF)).reshape(tile, comps)
                fold[i * frames : (i + 1) * frames, q : q + tile] = lax.dot_general(
                    now, hot, (((1,), (1,)), ((), ())), preferred_element_type=F32).astype(BF)
        out = jnp.dot(fold[...], temp[...], preferred_element_type=F32)
        lines = pl.ds(first, hg * frames)
        for q in range(planes):
            fbuf[q, lines, :] = fbuf[q, lines, :] - out[:, q * cols : (q + 1) * cols]

    def same_plane(n, carry):
        g = lax.div(n, nw)
        k = second(lax.rem(n, nw))
        zi = peer(k, -1)

        @pl.when(k > 0)
        def _():
            z2_copy(lax.max(k, 1), g).wait_recv()
            for dp in range(1, np_):
                x2_copy(dp, zi, g).start()

        model(p * nw + zi, g)
        return carry

    lax.fori_loop(0, groups * nw, same_plane, 0)

    def other_planes(n, carry):
        g = lax.div(n, (np_ - 1) * nw)
        dp = lax.rem(lax.div(n, nw), np_ - 1) + 1
        zi = peer(second(lax.rem(n, nw)), -1)
        x2_copy(dp, zi, g).wait_recv()
        model(lax.rem(p + np_ - dp, np_) * nw + zi, g)
        return carry

    lax.fori_loop(0, groups * (np_ - 1) * nw, other_planes, 0)

    for f in range(frames):
        for q in range(planes):
            one = fbuf[q, pl.ds(f, rows, stride=frames), :] * mask
            resid[f, pad : pad + rows, q * cols : (q + 1) * cols] = one.astype(BF)
    halo_start(resid, h2_s, h2_r)

    share = tr_out.shape[0]
    chosen = iota((share, comps), 1) == iota((share, comps), 0) + p * share
    chosen = jnp.where(chosen, 1.0, 0.0).astype(BF)
    for f in range(frames):
        one = tr32[pl.ds(f, rows, stride=frames), :].astype(BF)
        tt32[pl.ds(f, share, stride=frames), :] = lax.dot_general(
            chosen, one, (((1,), (1,)), ((), ())), preferred_element_type=F32)
    tr_out[...] = tt32[...].astype(BF).reshape(share, frames, rows)

    halo_wait(resid, h2_s, h2_r)

    def drained_planes(n, carry):
        dp, zi, g = lax.div(n, nw * groups) + 1, lax.rem(lax.div(n, groups), nw), lax.rem(n, groups)
        x1_copy(dp, zi, g).wait_send()
        x2_copy(dp, zi, g).wait_send()
        return carry

    lax.fori_loop(0, (np_ - 1) * nw * groups, drained_planes, 0)

    def drained_wide(n, carry):
        z2_copy(lax.div(n, groups) + 1, lax.rem(n, groups)).wait_send()
        return carry

    lax.fori_loop(0, (nw - 1) * groups, drained_wide, 0)


def back_kernel(tr_ref, resid, row_adj, col_adj, tr_hbm, back_hbm, back_out, out_s):
    planes, frames, rows, cols = back_out.shape
    tr_copy = pltpu.make_async_copy(tr_ref, tr_hbm, out_s.at[0])
    tr_copy.start()
    step = max(1, frames // 4)
    copies = []
    for f0 in range(0, frames, step):
        for f in range(f0, f0 + step):
            y = jnp.dot(row_adj[...], resid[f], preferred_element_type=F32).astype(BF)
            y = jnp.dot(y, col_adj[...], preferred_element_type=F32).astype(BF)
            for q in range(planes):
                back_out[q, f] = y[:, q * cols : (q + 1) * cols]
        copy = pltpu.make_async_copy(
            back_out.at[:, pl.ds(f0, step)], back_hbm.at[:, pl.ds(f0, step)], out_s.at[1 + f0 // step])
        copy.start()
        copies.append(copy)
    tr_copy.wait()
    for copy in copies:
        copy.wait()


def on_device(
    movie_frames, pixel_mask, tile_owner, support, templates, row_taps, col_taps, lag_gains, dilations
):
    planes, frames, rows, cols = movie_frames.shape
    np_ = lax.axis_size("planes")
    nw = lax.axis_size("wide")
    blocks = np_ * nw
    hb = rows // blocks
    groups = 1
    comps = support.shape[1]
    shapes = templates.shape[0]
    total = nw * frames
    pixels = planes * cols
    rim = (row_taps.shape[0] - 1) // 2
    pad = -(-rim // TILE) * TILE
    share = comps // np_
    piece = (hb, frames, comps)
    hbm = pl.BlockSpec(memory_space=pltpu.HBM)
    vm = pl.BlockSpec(memory_space=pltpu.VMEM)
    dma = pltpu.SemaphoreType.DMA
    middle = pl.pallas_call(
        whole_kernel,
        out_shape=(
            jax.ShapeDtypeStruct((share, frames, rows), BF),
            jax.ShapeDtypeStruct((frames, rows + 2 * pad, pixels), BF),
            jax.ShapeDtypeStruct((rows, rows + 2 * pad), BF),
            jax.ShapeDtypeStruct((pixels, pixels), BF),
        ),
        in_specs=[hbm] * 9,
        out_specs=(vm,) * 4,
        scratch_shapes=[
            pltpu.VMEM(movie_frames.shape, BF),
            pltpu.VMEM((shapes * planes, cols), BF),
            pltpu.VMEM(support.shape, I32),
            pltpu.VMEM(pixel_mask.shape, I32),
            pltpu.SMEM((rows,), I32),
            pltpu.SMEM(row_taps.shape, F32),
            pltpu.SMEM(col_taps.shape, F32),
            pltpu.VMEM((lag_gains.shape[1], 1, lag_gains.shape[2]), F32),
            pltpu.SMEM((dilations.shape[1],), I32),
            pltpu.VMEM((shapes * planes, cols), F32),
            pltpu.VMEM((shapes, pixels), BF),
            pltpu.VMEM((pixels, shapes), BF),
            pltpu.VMEM((pixels, pixels), BF),
            pltpu.VMEM((rows, rows + 2 * pad), BF),
            pltpu.VMEM((total, total), BF),
            pltpu.VMEM((frames, rows + 2 * pad, pixels), BF),
            pltpu.VMEM((planes, rows * frames, cols), F32),
            pltpu.VMEM((hb // groups * frames, shapes), F32),
            pltpu.VMEM((blocks,) + piece, BF),
            pltpu.VMEM(((np_ - 1) * nw,) + piece, BF),
            pltpu.VMEM((nw,) + piece, BF),
            pltpu.VMEM((nw,) + piece, BF),
            pltpu.VMEM((nw, total, total), BF),
            pltpu.VMEM((nw,) + piece, BF),
            pltpu.VMEM((blocks,) + piece, BF),
            pltpu.VMEM((rows * frames, comps), F32),
            pltpu.VMEM((share * frames, rows), F32),
            pltpu.VMEM((hb // groups * frames, shapes), BF),
            dma((9,)), pltpu.SemaphoreType.REGULAR((2, max(1, nw - 2))), dma((2,)), dma((2,)), dma((2,)), dma((2,)),
            dma((nw - 1,)), dma((nw - 1,)),
            dma(((np_ - 1) * nw * groups,)), dma(((np_ - 1) * nw * groups,)),
            dma(((nw - 1) * groups,)), dma(((nw - 1) * groups,)),
            dma(((nw - 1) * groups,)), dma(((nw - 1) * groups,)),
            dma(((np_ - 1) * nw * groups,)), dma(((np_ - 1) * nw * groups,)),
        ],
        compiler_params=pltpu.CompilerParams(
            collective_id=0, has_side_effects=True, vmem_limit_bytes=40 * 1024 * 1024
        ),
    )(*[pltpu.with_memory_space_constraint(x, pltpu.HBM) for x in (
        movie_frames, templates.reshape(shapes * planes, cols), support, pixel_mask, tile_owner[:, 0],
        row_taps, col_taps, jnp.transpose(lag_gains, (1, 0, 2)), dilations[0],
    )])
    return pl.pallas_call(
        back_kernel,
        out_shape=(
            jax.ShapeDtypeStruct((share, frames, rows), BF),
            jax.ShapeDtypeStruct(movie_frames.shape, BF),
        ),
        in_specs=[vm] * 4,
        out_specs=(hbm, hbm),
        scratch_shapes=[pltpu.VMEM(movie_frames.shape, BF), dma((5,))],
        compiler_params=pltpu.CompilerParams(vmem_limit_bytes=16 * 1024 * 1024),
    )(*middle)


def solution(mesh):
    return jax.shard_map(
        on_device,
        mesh=mesh,
        in_specs=(
            P("planes", ("groups", "wide"), "rep", None),
            P("rep", None),
            P("rep", None),
            P("rep", None),
            P(None, "planes", None),
            P(),
            P(),
            P("wide", None, None),
            P("wide", None),
        ),
        out_specs=(
            P("planes", ("groups", "wide"), "rep"),
            P("planes", ("groups", "wide"), "rep", None),
        ),
        check_vma=False,
    )
```
